256 devices in a mesh: group: 8 (over x, core), member: 32 (over y, z).
Axes of the slice: x: 4, y: 4, z: 8, core: 2. Of those that a mesh axis runs over, the one named last changes fastest.
Arguments:
- q_rows: bfloat16 [65536, 8192], P(('group', 'member')), may hold values from -36 to 36
- own_kv: bfloat16 [65536, 1024], P(('group', 'member')), may hold values from -6 to 6
- cache: bfloat16 [1024, 64, 1024], P(('group', 'member')), may hold values from -6 to 6
- recomp_hidden: bfloat16 [512, 8, 16, 4096], P(('group', 'member')), may hold values from -6 to 6
- w_kv: bfloat16 [4096, 1024], P('member', 'group'), may hold values from -0.09375 to 0.09375
- retrieval: int32 [512, 8], P(('group', 'member')), may hold values from 0 to 127, as said below
- positions: int32 [512, 8, 16], P(('group', 'member')), may hold values from 0 to 63, as said below
Outputs:
- attn_out: bfloat16 [65536, 8192], P(('group', 'member'))
The draws below stay inside these ranges and needn't reach their ends.
Inputs may be any that keep to these rules, and one draw needn't show every extreme that they name: `retrieval`: the 8 passages of one query are different. Passage i of a group's corpus is held by the device of member index i // 4 in that group. The queries of one device name at most 1 passages held by any one device, and this bound is reached. The 16 positions of one retrieved passage are different.
All inputs are finite; a program needn't handle non-finite values.
Results may differ from the reference program's by a relative error of at most 0.0054.
Values may be sent and summed in bfloat16 or wider, within the bound.
A program may use at most 128 MiB of HBM per device.

```python
import jax
import jax.numpy as jnp
from jax import lax

D = 4096
HQ = 64
KVH = 4
HD = 128
TOPP = 8
QLEN = 128
Q_DEV = 2
PLEN = 64
PASS_DEV = 4
RECOMP = 16
OWNERS = 32
GROUPS = 8
QUERIES = 512
PASSAGES = 1024
N_MEMBER = 32


def draw_q_rows(key, part):
    total_rows = QLEN * QUERIES
    result = jnp.clip(jax.random.normal(jax.random.fold_in(key, 1), (total_rows, HQ * HD), jnp.float32), -6.0, 6.0)
    return result.astype(jnp.bfloat16)


def draw_own_kv(key, part):
    total_rows = QLEN * QUERIES
    half_width = KVH * HD
    result = jnp.clip(jax.random.normal(jax.random.fold_in(key, 2), (total_rows, 2 * half_width), jnp.float32), -6.0, 6.0)
    return result.astype(jnp.bfloat16)


def draw_retrieval(key, part):
    requests = Q_DEV * TOPP
    copies = (requests + OWNERS - 1) // OWNERS

    def per_device(device):
        device_key = jax.random.fold_in(key, device)
        hottest = jax.random.randint(jax.random.fold_in(key, 100003 + device // OWNERS), (), 0, OWNERS).astype(jnp.int32)
        sequence = []
        for copy_index in range(copies):
            shuffled = jax.random.permutation(jax.random.fold_in(device_key, copy_index), OWNERS - 1).astype(jnp.int32)
            others = shuffled + (shuffled >= hottest).astype(jnp.int32)
            sequence.append(jnp.concatenate([hottest.reshape(1), others]))
        holders = jnp.concatenate(sequence)[:requests]
        repeats = (jnp.arange(requests) // OWNERS).astype(jnp.int32)
        offsets = jax.random.randint(jax.random.fold_in(device_key, 5000), (OWNERS,), 0, PASS_DEV).astype(jnp.int32)
        inside = (offsets[holders] + repeats) % PASS_DEV
        chosen = holders * PASS_DEV + inside
        mixing = jax.random.permutation(jax.random.fold_in(device_key, 6000), requests)
        return chosen[mixing].reshape(Q_DEV, TOPP)
    drawn = jax.vmap(per_device)(jnp.arange(GROUPS * OWNERS).astype(jnp.int32))
    return drawn.reshape(QUERIES, TOPP).astype(jnp.int32)


def draw_positions(key, part):
    count = QUERIES * TOPP
    split_keys = jax.random.split(key, count)
    picks = jax.vmap(lambda one_key: jax.random.permutation(one_key, PLEN)[:RECOMP])(split_keys)
    return picks.reshape(QUERIES, TOPP, RECOMP).astype(jnp.int32)


def level_of(stream_key, dims, cuts, smallest, largest):
    factor_of, own = 1.0, jax.random.fold_in(stream_key, 6)
    for position, blocks in cuts:
        draws = jnp.exp(jax.random.uniform(jax.random.fold_in(own, position), (blocks,), jnp.float32, smallest / len(cuts), largest / len(cuts)))
        factor_of = factor_of * jnp.repeat(draws, dims[position] // blocks).reshape([-1 if axis == position else 1 for axis in range(len(dims))])
    return factor_of


def gaussian(rng, extent, spread, most, cuts=(), held_as=jnp.bfloat16):
    values = jax.random.normal(rng, extent, jnp.float32) * spread
    if len(cuts) > 0:
        values = level_of(rng, extent, cuts, -0.22, 0.18) * values
    return jnp.clip(values, min=-most, max=most).astype(held_as)


def setup_inputs(seed: int = 0) -> dict:
    key_list = jax.random.split(jax.random.key(seed), 8)
    return {
        "q_rows": draw_q_rows(jax.random.fold_in(key_list[7], 71), 0),
        "own_kv": draw_own_kv(jax.random.fold_in(key_list[7], 71), 0),
        "cache": gaussian(key_list[2], (PASSAGES, PLEN, 2 * KVH * HD), 1.0, 6.0, ((0, 256),)),
        "recomp_hidden": gaussian(key_list[3], (QUERIES, TOPP, RECOMP, D), 1.0, 6.0, ((0, 256),)),
        "w_kv": gaussian(key_list[4], (D, 2 * KVH * HD), D ** -0.5, 0.09375, ((0, 32), (1, 8))),
        "retrieval": draw_retrieval(jax.random.fold_in(key_list[7], 71), 0),
        "positions": draw_positions(jax.random.fold_in(key_list[7], 71), 0),
    }


EPSILON = 1e-06

def reference(q_rows, own_kv, cache, recomp_hidden, w_kv, retrieval, positions):
    query_count = retrieval.shape[0]
    per_group = Q_DEV * N_MEMBER
    corpus_size = PASS_DEV * N_MEMBER
    kv_width = 2 * KVH * HD
    grouped = HQ // KVH
    span_keys = TOPP * PLEN + QLEN
    scale = 1.0 / HD ** 0.5
    weights_full = w_kv.astype(jnp.float32)
    query_all = q_rows.reshape(query_count, QLEN, KVH, grouped, HD)
    own_all = own_kv.reshape(query_count, QLEN, kv_width)
    token_pos = jnp.arange(QLEN)[:, None]
    key_pos = jnp.arange(span_keys)[None, :]
    visible = (key_pos < TOPP * PLEN) | (key_pos - TOPP * PLEN <= token_pos)

    def one_query(query_index):
        group_index = query_index // per_group
        passage_ids = (group_index * corpus_size + retrieval[query_index]).astype(jnp.int32)
        blocks = cache[passage_ids].astype(jnp.float32)
        hidden = recomp_hidden[query_index].astype(jnp.float32)
        normed = (hidden * lax.rsqrt(lax.optimization_barrier(jnp.mean(hidden * hidden, axis=-1, keepdims=True)) + EPSILON)).astype(jnp.bfloat16)
        recomputed = jnp.einsum('jrd,de->jre', normed.astype(jnp.float32), weights_full).astype(jnp.bfloat16)
        onehot = positions[query_index][:, :, None] == jnp.arange(PLEN)[None, None, :]
        covered = jnp.any(onehot, axis=1)
        placed = jnp.einsum('jrp,jre->jpe', onehot.astype(jnp.float32), recomputed.astype(jnp.float32))
        context = jnp.where(covered[:, :, None], placed, blocks).astype(jnp.bfloat16)
        context = jnp.concatenate([context.reshape(TOPP * PLEN, kv_width), own_all[query_index]], axis=0)
        keys = context[:, :KVH * HD].reshape(span_keys, KVH, HD).astype(jnp.float32)
        values = context[:, KVH * HD:].reshape(span_keys, KVH, HD).astype(jnp.float32)
        queries = query_all[query_index].astype(jnp.float32)
        scores = jnp.einsum('tkgd,skd->kgts', queries, keys) * scale
        scores = jnp.where(visible, scores, -jnp.inf)
        peak = lax.optimization_barrier(jnp.max(scores, axis=-1, keepdims=True))
        expd = jnp.exp(scores - peak)
        probs = (expd / lax.optimization_barrier(jnp.sum(expd, axis=-1, keepdims=True))).astype(jnp.bfloat16)
        output = jnp.einsum('kgts,skd->tkgd', probs.astype(jnp.float32), values)
        return output.astype(jnp.bfloat16).reshape(QLEN, HQ * HD)
    results = lax.map(one_query, jnp.arange(query_count).astype(jnp.int32))
    return results.reshape(query_count * QLEN, HQ * HD)
```

```python
import functools

import jax
import jax.numpy as jnp
from jax import lax
from jax.experimental import pallas as pl
from jax.experimental.pallas import tpu as pltpu
from jax.sharding import PartitionSpec as P

D = 4096
HQ = 64
KVH = 4
HD = 128
TOPP = 8
QLEN = 128
PLEN = 64
RECOMP = 16
KEPT = PLEN - RECOMP
EPSILON = 1e-06
LOG2E = 1.4426950408889634
MESH = pl.DeviceIdType.MESH
NX, NY, NZ = 4, 4, 8
HPB = 2


def comm_kernel(
    cache_ref, hid_ref, w_ref, pos_ref, ret_ref,
    slots_ref, rec_ref,
    blk, wb, hn, acc, stage, recst, info,
    local_sem, wz_s, wz_r, wy_s, wy_r, wx_s, wx_r, wf_s, wf_r,
    in_s, in_r, zr_s, zr_r, zl_s, zl_r, ys_s, ys_r, hx_s, hx_r, rx_s, rx_r,
):
    g, m = lax.axis_index("group"), lax.axis_index("member")
    x, c, y, z = g // 2, g % 2, m // NZ, m % NZ

    def at(dx=0, dc=0, dy=0, dz=0):
        gg = ((x + dx + NX) % NX) * 2 + (c + dc) % 2
        return gg, ((y + dy + NY) % NY) * NZ + (z + dz + NZ) % NZ

    def remote(src, dst, s, r, dev):
        return pltpu.make_async_remote_copy(
            src_ref=src, dst_ref=dst, send_sem=s, recv_sem=r, device_id=dev, device_id_type=MESH
        )

    sends = []

    def go(copy):
        copy.start()
        sends.append(copy)
        return copy

    peers = [at(dz=k) for k in range(1, NZ)] + [at(dy=k) for k in range(1, NY)]
    peers += [at(dx=1), at(dx=-1), at(dc=1)]
    barrier = pltpu.get_barrier_semaphore()
    for dev in peers:
        pl.semaphore_signal(barrier, inc=1, device_id=dev, device_id_type=MESH)

    lane = lax.broadcasted_iota(jnp.int32, (16, 256), 1)
    row = lane % PLEN
    spots = pos_ref[...].reshape(16, RECOMP)
    covered = row == spots[:, 0:1]
    for j in range(1, RECOMP):
        covered = covered | (row == spots[:, j : j + 1])
    free = jnp.where(covered[:, :PLEN], 0.0, 1.0).astype(jnp.bfloat16)
    below = lax.broadcasted_iota(jnp.int32, (PLEN, 256), 0)
    before = below < lax.broadcasted_iota(jnp.int32, (PLEN, 256), 1) % PLEN
    rank = jnp.dot(
        free, jnp.where(before, 1.0, 0.0).astype(jnp.bfloat16), preferred_element_type=jnp.float32
    )
    wanted = ret_ref[...]
    keep = jnp.logical_not(covered) & (lane // PLEN == wanted % 4)
    info[0, :, 0:256] = jnp.where(keep, rank, -1.0)
    info[0, :, 256:512] = jnp.broadcast_to((wanted // 4).astype(jnp.float32), (16, 256))

    pl.semaphore_wait(barrier, len(peers))

    zrow = pl.multiple_of(z * 128, 128)
    for k in range(1, NZ):
        go(remote(w_ref, wb.at[x, y, pl.ds(zrow, 128)], wz_s.at[k], wz_r.at[k], at(dz=k)))
    for k in range(1, NY):
        go(remote(info.at[0], info.at[k], in_s.at[k], in_r.at[k], at(dy=k)))

    def half_right(i):
        return 0 if i == 6 else i % 2

    def half_left(i):
        return 1 if i == 6 else 1 - i % 2

    def zz(d):
        return (z + d + NZ) % NZ

    def right(i):
        h = half_right(i)
        src = cache_ref.at[h] if i < 2 else blk.at[zz(-(i // 2)), h]
        return remote(src, blk.at[zz(-(i // 2)), h], zr_s.at[i], zr_r.at[i], at(dz=1))

    def left(i):
        h = half_left(i)
        src = cache_ref.at[h] if i < 2 else blk.at[zz(i // 2), h]
        return remote(src, blk.at[zz(i // 2), h], zl_s.at[i], zl_r.at[i], at(dz=-1))

    def z_arrived(i):
        d = blk.at[zz(-1 - i // 2), half_right(i)]
        remote(d, d, zr_s.at[i], zr_r.at[i], at(dz=-1)).wait_recv()
        if i + 2 <= 6:
            go(right(i + 2))
        d = blk.at[zz(1 + i // 2), half_left(i)]
        remote(d, d, zl_s.at[i], zl_r.at[i], at(dz=1)).wait_recv()
        if i + 2 <= 6:
            go(left(i + 2))

    for i in range(2):
        go(right(i))
        go(left(i))
    own_block = pltpu.make_async_copy(cache_ref, blk.at[z], local_sem.at[0])
    own_block.start()
    own_w = pltpu.make_async_copy(w_ref, wb.at[x, y, pl.ds(zrow, 128)], local_sem.at[1])
    own_w.start()

    def norm(i, carry):
        rows = pl.ds(pl.multiple_of(i * 32, 32), 32)
        h = hid_ref[rows, :].astype(jnp.float32)
        inv = lax.rsqrt(jnp.mean(h * h, axis=1, keepdims=True) + EPSILON)
        n = (h * inv).astype(jnp.bfloat16)
        for b in range(4):
            hn[b, rows, :] = n[:, b * 1024 : (b + 1) * 1024]
        return carry

    lax.fori_loop(0, 8, norm, 0)
    mine, theirs = pl.ds(0, 256), pl.ds(256, 256)
    go(remote(hn.at[:, mine], hn.at[:, theirs], hx_s, hx_r, at(dc=1)))

    local = []

    def select(d):
        holder = zz(d)
        name = (y * NZ + holder).astype(jnp.float32)
        want = lax.broadcasted_iota(jnp.int32, (KEPT, 256), 0).astype(jnp.float32)
        picks = []
        for k in range(NY):
            hit = info[k, :, 256:512] == name
            v = jnp.max(jnp.where(hit, info[k, :, 0:256], -1.0), axis=0, keepdims=True)
            picks.append(jnp.where(want == v, 1.0, 0.0).astype(jnp.bfloat16))
        got = jnp.dot(
            jnp.concatenate(picks, axis=0),
            blk[holder].reshape(256, 1024),
            preferred_element_type=jnp.float32,
        ).astype(jnp.bfloat16)
        for k in range(NY):
            stage[k, d] = got[k * KEPT : (k + 1) * KEPT]
        slot = slots_ref.at[y * NZ + holder]
        for k in range(1, NY):
            go(remote(stage.at[k, d], slot, ys_s.at[k, d], ys_r.at[k, d], at(dy=-k)))
        mine_too = pltpu.make_async_copy(stage.at[0, d], slot, local_sem.at[4 + d])
        mine_too.start()
        local.append(mine_too)

    started = set()

    def project(dx, k):
        xi, yi = (x + dx + NX) % NX, (y - k + NY) % NY
        part = jnp.dot(hn[yi], wb[xi, yi], preferred_element_type=jnp.float32)
        if dx in started:
            acc[dx] = acc[dx] + part
        else:
            started.add(dx)
            acc[dx] = part

    def chunk(dx, k):
        return wb.at[(x + dx + NX) % NX, (y - k + NY) % NY]

    def wx_send(k):
        go(remote(chunk(0, k), chunk(0, k), wx_s.at[0, k], wx_r.at[0, k], at(dx=1)))
        go(remote(chunk(0, k), chunk(0, k), wx_s.at[1, k], wx_r.at[1, k], at(dx=-1)))

    def wx_arrived(k):
        d = chunk(-1, k)
        remote(d, d, wx_s.at[0, k], wx_r.at[0, k], at(dx=-1)).wait_recv()
        if k in (0, 1):
            go(remote(d, d, wf_s.at[k], wf_r.at[k], at(dx=1)))
        d = chunk(1, k)
        remote(d, d, wx_s.at[1, k], wx_r.at[1, k], at(dx=1)).wait_recv()
        if k in (2, 3):
            go(remote(d, d, wf_s.at[k], wf_r.at[k], at(dx=-1)))
        project(3, k)
        project(1, k)

    def wf_arrived(k):
        d = chunk(2, k)
        remote(d, d, wf_s.at[k], wf_r.at[k], at(dx=-1 if k in (0, 1) else 1)).wait_recv()
        project(2, k)

    def wy_arrived(k):
        d = chunk(0, k)
        remote(d, d, wy_s.at[k], wy_r.at[k], at(dy=-k)).wait_recv()
        wx_send(k)
        project(0, k)

    for k in range(1, NY):
        remote(info.at[k], info.at[k], in_s.at[k], in_r.at[k], at(dy=-k)).wait_recv()
    own_block.wait()
    select(0)

    own_w.wait()
    for k in range(1, NZ):
        d = wb.at[x, y, pl.ds(pl.multiple_of(zz(-k) * 128, 128), 128)]
        remote(d, d, wz_s.at[k], wz_r.at[k], at(dz=-k)).wait_recv()
    wx_send(0)
    for k in range(1, NY):
        go(remote(chunk(0, 0), chunk(0, 0), wy_s.at[k], wy_r.at[k], at(dy=k)))
    remote(hn.at[:, mine], hn.at[:, theirs], hx_s, hx_r, at(dc=1)).wait_recv()
    project(0, 0)

    z_arrived(0)
    wx_arrived(0)
    wy_arrived(1)
    wy_arrived(3)
    z_arrived(1)
    select(7)
    select(1)
    wy_arrived(2)
    wf_arrived(0)
    z_arrived(2)
    wx_arrived(1)
    z_arrived(3)
    select(6)
    select(2)
    wx_arrived(3)
    z_arrived(4)
    wx_arrived(2)
    wf_arrived(1)
    wf_arrived(3)
    z_arrived(5)
    select(5)
    select(3)
    wf_arrived(2)

    for dx in range(NX):
        xi = (x + dx) % NX
        recst[dx] = acc[dx].astype(jnp.bfloat16)
        dst = rec_ref.at[2 * xi + c]
        go(remote(recst.at[dx, theirs], dst, rx_s.at[dx], rx_r.at[dx], at(dc=1)))
        own = pltpu.make_async_copy(recst.at[dx, mine], dst, local_sem.at[12 + dx])
        own.start()
        local.append(own)

    z_arrived(6)
    select(4)

    for k in range(1, NY):
        for d in range(NZ):
            slot = slots_ref.at[((y + k) % NY) * NZ + zz(d)]
            remote(stage.at[k, d], slot, ys_s.at[k, d], ys_r.at[k, d], at(dy=k)).wait_recv()
    for dx in range(NX):
        dst = rec_ref.at[2 * ((x + dx) % NX) + (c + 1) % 2]
        remote(recst.at[dx, theirs], dst, rx_s.at[dx], rx_r.at[dx], at(dc=1)).wait_recv()
    for copy in local:
        copy.wait()
    for copy in sends:
        copy.wait_send()


def attend_kernel(holder_ref, q_ref, own_ref, slots_ref, rec_k_ref, rec_v_ref, out_ref, keys, vals):
    n, h = pl.program_id(0), pl.program_id(1)
    kcol = pl.multiple_of(h * HD, HD)
    vcol = pl.multiple_of(KVH * HD + h * HD, HD)
    cached, span = TOPP * KEPT, TOPP * PLEN + QLEN
    for j in range(TOPP):
        s = holder_ref[n, j]
        keys[j * KEPT : (j + 1) * KEPT, :] = slots_ref[s, :, pl.ds(kcol, HD)]
        vals[j * KEPT : (j + 1) * KEPT, 0:HD] = slots_ref[s, :, pl.ds(vcol, HD)]
    keys[cached : TOPP * PLEN, :] = rec_k_ref[0]
    vals[cached : TOPP * PLEN, 0:HD] = rec_v_ref[0]
    keys[TOPP * PLEN :, :] = own_ref[:, pl.ds(kcol, HD)]
    vals[TOPP * PLEN :, 0:HD] = own_ref[:, pl.ds(vcol, HD)]
    vals[:, HD:] = jnp.ones((span, HD), jnp.bfloat16)

    t = lax.broadcasted_iota(jnp.int32, (HPB * QLEN, QLEN), 0) % QLEN
    seen = lax.broadcasted_iota(jnp.int32, (HPB * QLEN, QLEN), 1) <= t
    factor = LOG2E / HD**0.5

    for b in range(HQ // KVH // HPB):
        heads = [b * HPB + i for i in range(HPB)]
        q = jnp.concatenate([q_ref[:, i * HD : (i + 1) * HD] for i in heads], axis=0)
        s = lax.dot_general(
            q, keys[...], (((1,), (1,)), ((), ())), preferred_element_type=jnp.float32
        )
        s_own = jnp.where(seen, s[:, TOPP * PLEN :], -jnp.inf)
        s = jnp.concatenate([s[:, : TOPP * PLEN], s_own], axis=1)
        peak = jnp.max(s, axis=1, keepdims=True)
        p = jnp.exp2((s - peak) * factor).astype(jnp.bfloat16)
        o = jnp.dot(p, vals[...], preferred_element_type=jnp.float32)
        o = (o[:, :HD] / o[:, HD:]).astype(jnp.bfloat16)
        for i, hd in enumerate(heads):
            out_ref[:, hd * HD : (hd + 1) * HD] = o[i * QLEN : (i + 1) * QLEN]


def communicate(cache, hidden, w_kv, positions, wanted):
    dma, bf, f32 = pltpu.SemaphoreType.DMA, jnp.bfloat16, jnp.float32
    vmem, hbm = pl.BlockSpec(memory_space=pltpu.VMEM), pl.BlockSpec(memory_space=pl.ANY)
    return pl.pallas_call(
        comm_kernel,
        out_shape=(
            jax.ShapeDtypeStruct((NY * NZ, KEPT, 1024), bf),
            jax.ShapeDtypeStruct((8, 256, 128), bf),
        ),
        in_specs=[hbm, vmem, vmem, vmem, vmem],
        out_specs=(hbm, hbm),
        scratch_shapes=[
            pltpu.VMEM((NZ, 2, 128, 1024), bf),
            pltpu.VMEM((NX, NY, 1024, 128), bf),
            pltpu.VMEM((4, 512, 1024), bf),
            pltpu.VMEM((NX, 512, 128), f32),
            pltpu.VMEM((NY, NZ, KEPT, 1024), bf),
            pltpu.VMEM((NX, 512, 128), bf),
            pltpu.VMEM((NY, 16, 512), f32),
            dma((16,)),
            dma((NZ,)), dma((NZ,)), dma((NY,)), dma((NY,)),
            dma((2, NY)), dma((2, NY)), dma((NY,)), dma((NY,)),
            dma((NY,)), dma((NY,)), dma((7,)), dma((7,)), dma((7,)), dma((7,)),
            dma((NY, NZ)), dma((NY, NZ)), dma, dma, dma((NX,)), dma((NX,)),
        ],
        compiler_params=pltpu.CompilerParams(
            collective_id=0, has_side_effects=True, vmem_limit_bytes=48 << 20
        ),
        name="exchange",
    )(cache, hidden, w_kv, positions, wanted)


def attend(holders, q, own, slots, rec):
    width = HQ // KVH * HD
    return pl.pallas_call(
        attend_kernel,
        out_shape=jax.ShapeDtypeStruct(q.shape, q.dtype),
        grid_spec=pltpu.PrefetchScalarGridSpec(
            num_scalar_prefetch=1,
            grid=(q.shape[0] // QLEN, KVH),
            in_specs=[
                pl.BlockSpec((QLEN, width), lambda n, h, s: (n, h)),
                pl.BlockSpec((QLEN, 1024), lambda n, h, s: (n, 0)),
                pl.BlockSpec((NY * NZ, KEPT, 1024), lambda n, h, s: (0, 0, 0)),
                pl.BlockSpec((1, QLEN, HD), lambda n, h, s: (h, n, 0)),
                pl.BlockSpec((1, QLEN, HD), lambda n, h, s: (h + KVH, n, 0)),
            ],
            out_specs=pl.BlockSpec((QLEN, width), lambda n, h, s: (n, h)),
            scratch_shapes=[
                pltpu.VMEM((TOPP * PLEN + QLEN, HD), jnp.bfloat16),
                pltpu.VMEM((TOPP * PLEN + QLEN, 2 * HD), jnp.bfloat16),
            ],
        ),
        compiler_params=pltpu.CompilerParams(vmem_limit_bytes=48 << 20),
        name="attend",
    )(holders, q, own, slots, rec, rec)


def local(q_rows, own_kv, cache, recomp_hidden, w_kv, retrieval, positions):
    slots, rec = communicate(
        cache.reshape(2, 128, 1024),
        recomp_hidden.reshape(256, D),
        w_kv,
        positions,
        retrieval.reshape(16, 1),
    )
    return attend(retrieval // 4, q_rows, own_kv, slots, rec)


def solution(mesh):
    both = ("group", "member")
    placed = (
        P(both, None),
        P(both, None),
        P(both, None, None),
        P(both, None, None, None),
        P("member", "group"),
        P(both, None),
        P(both, None, None),
    )
    return jax.shard_map(
        local, mesh=mesh, in_specs=placed, out_specs=P(both, None), check_vma=False
    )
```

```python
import functools

import jax
import jax.numpy as jnp
from jax import lax
from jax.experimental import pallas as pl
from jax.experimental.pallas import tpu as pltpu
from jax.sharding import PartitionSpec as P

D = 4096
HQ = 64
KVH = 4
HD = 128
TOPP = 8
QLEN = 128
PLEN = 64
RECOMP = 16
KEPT = PLEN - RECOMP
EPSILON = 1e-06
LOG2E = 1.4426950408889634
MESH = pl.DeviceIdType.MESH
NX, NY, NZ = 4, 4, 8
HPB = 8
GROUPED = HQ // KVH
WIDTH = GROUPED * HD
FACTOR = LOG2E / HD**0.5


def comm_kernel(
    ret_ref, cache_ref, hid_hbm, w_ref, pos_hbm, q_hbm, own_hbm,
    slots_ref, rec_ref, part_ref, lse_ref,
    blk, wb, hn, acc, stage, recst, info, hid_ref, pos_ref, queries, own_ref, ones, part, lse,
    local_sem, in_sem, q_sem, part_sem, lse_sem, wz_s, wz_r, wy_s, wy_r, wx_s, wx_r, wf_s, wf_r,
    in_s, in_r, zr_s, zr_r, zl_s, zl_r, ys_s, ys_r, hx_s, hx_r, rx_s, rx_r,
):
    g, m = lax.axis_index("group"), lax.axis_index("member")
    x, c, y, z = g // 2, g % 2, m // NZ, m % NZ

    def at(dx=0, dc=0, dy=0, dz=0):
        gg = ((x + dx + NX) % NX) * 2 + (c + dc) % 2
        return gg, ((y + dy + NY) % NY) * NZ + (z + dz + NZ) % NZ

    def remote(src, dst, s, r, dev):
        return pltpu.make_async_remote_copy(
            src_ref=src, dst_ref=dst, send_sem=s, recv_sem=r, device_id=dev, device_id_type=MESH
        )

    sends = []

    def go(copy):
        copy.start()
        sends.append(copy)
        return copy

    loads = [
        pltpu.make_async_copy(src, dst, in_sem.at[i])
        for i, (src, dst) in enumerate(((pos_hbm, pos_ref), (own_hbm, own_ref), (hid_hbm, hid_ref)))
    ]

    def query(n, h):
        block = (pl.ds(n * QLEN, QLEN), pl.ds(h * WIDTH, WIDTH))
        return pltpu.make_async_copy(q_hbm.at[block], queries.at[block], q_sem.at[n, h])

    peers = [at(dz=k) for k in range(1, NZ)] + [at(dy=k) for k in range(1, NY)]
    peers += [at(dx=1), at(dx=-1), at(dc=1)]
    barrier = pltpu.get_barrier_semaphore()
    for dev in peers:
        pl.semaphore_signal(barrier, inc=1, device_id=dev, device_id_type=MESH)

    for copy in loads:
        copy.start()
    for n in range(2):
        for h in range(KVH):
            query(n, h).start()

    lane = lax.broadcasted_iota(jnp.int32, (16, 256), 1)
    row = lane % PLEN
    loads[0].wait()
    spots = pos_ref[...].reshape(16, RECOMP)
    covered = row == spots[:, 0:1]
    for j in range(1, RECOMP):
        covered = covered | (row == spots[:, j : j + 1])
    free = jnp.where(covered[:, :PLEN], 0.0, 1.0).astype(jnp.bfloat16)
    below = lax.broadcasted_iota(jnp.int32, (PLEN, 256), 0)
    before = below < lax.broadcasted_iota(jnp.int32, (PLEN, 256), 1) % PLEN
    rank = jnp.dot(
        free, jnp.where(before, 1.0, 0.0).astype(jnp.bfloat16), preferred_element_type=jnp.float32
    )
    request = lax.broadcasted_iota(jnp.int32, (16, 256), 0)
    wanted = jnp.zeros((16, 256), jnp.int32)
    for k in range(16):
        wanted = jnp.where(request == k, ret_ref[k // TOPP, k % TOPP], wanted)
    keep = jnp.logical_not(covered) & (lane // PLEN == wanted % 4)
    info[0, :, 0:256] = jnp.where(keep, rank, -1.0)
    info[0, :, 256:512] = (wanted // 4).astype(jnp.float32)

    pl.semaphore_wait(barrier, len(peers))

    zrow = pl.multiple_of(z * 128, 128)
    for k in range(1, NZ):
        go(remote(w_ref, wb.at[x, y, pl.ds(zrow, 128)], wz_s.at[k], wz_r.at[k], at(dz=k)))
    for k in range(1, NY):
        go(remote(info.at[0], info.at[k], in_s.at[k], in_r.at[k], at(dy=k)))

    def half_right(i):
        return 0 if i == 6 else i % 2

    def half_left(i):
        return 1 if i == 6 else 1 - i % 2

    def zz(d):
        return (z + d + NZ) % NZ

    def right(i):
        h = half_right(i)
        src = cache_ref.at[h] if i < 2 else blk.at[zz(-(i // 2)), h]
        return remote(src, blk.at[zz(-(i // 2)), h], zr_s.at[i], zr_r.at[i], at(dz=1))

    def left(i):
        h = half_left(i)
        src = cache_ref.at[h] if i < 2 else blk.at[zz(i // 2), h]
        return remote(src, blk.at[zz(i // 2), h], zl_s.at[i], zl_r.at[i], at(dz=-1))

    def z_arrived(i):
        d = blk.at[zz(-1 - i // 2), half_right(i)]
        remote(d, d, zr_s.at[i], zr_r.at[i], at(dz=-1)).wait_recv()
        if i + 2 <= 6:
            go(right(i + 2))
        d = blk.at[zz(1 + i // 2), half_left(i)]
        remote(d, d, zl_s.at[i], zl_r.at[i], at(dz=1)).wait_recv()
        if i + 2 <= 6:
            go(left(i + 2))

    for i in range(2):
        go(right(i))
        go(left(i))
    own_block = pltpu.make_async_copy(cache_ref, blk.at[z], local_sem.at[0])
    own_block.start()
    own_w = pltpu.make_async_copy(w_ref, wb.at[x, y, pl.ds(zrow, 128)], local_sem.at[1])
    own_w.start()

    loads[2].wait()
    def norm(i, carry):
        rows = pl.ds(pl.multiple_of(i * 32, 32), 32)
        h = hid_ref[rows, :].astype(jnp.float32)
        inv = lax.rsqrt(jnp.mean(h * h, axis=1, keepdims=True) + EPSILON)
        n = (h * inv).astype(jnp.bfloat16)
        for b in range(4):
            hn[b, rows, :] = n[:, b * 1024 : (b + 1) * 1024]
        return carry

    lax.fori_loop(0, 8, norm, 0)
    mine, theirs = pl.ds(0, 256), pl.ds(256, 256)
    go(remote(hn.at[:, mine], hn.at[:, theirs], hx_s, hx_r, at(dc=1)))

    local = []

    def select(d):
        holder = zz(d)
        name = (y * NZ + holder).astype(jnp.float32)
        want = lax.broadcasted_iota(jnp.int32, (KEPT, 256), 0).astype(jnp.float32)
        picks = []
        for k in range(NY):
            hit = info[k, :, 256:512] == name
            v = jnp.max(jnp.where(hit, info[k, :, 0:256], -1.0), axis=0, keepdims=True)
            picks.append(jnp.where(want == v, 1.0, 0.0).astype(jnp.bfloat16))
        got = jnp.dot(
            jnp.concatenate(picks, axis=0),
            blk[holder].reshape(256, 1024),
            preferred_element_type=jnp.float32,
        ).astype(jnp.bfloat16)
        for k in range(NY):
            stage[k, d] = got[k * KEPT : (k + 1) * KEPT]
        slot = slots_ref.at[y * NZ + holder]
        for k in range(1, NY):
            go(remote(stage.at[k, d], slot, ys_s.at[k, d], ys_r.at[k, d], at(dy=-k)))
        mine_too = pltpu.make_async_copy(stage.at[0, d], slot, local_sem.at[4 + d])
        mine_too.start()
        local.append(mine_too)

    started = set()

    def project(dx, k):
        xi, yi = (x + dx + NX) % NX, (y - k + NY) % NY
        part = jnp.dot(hn[yi], wb[xi, yi], preferred_element_type=jnp.float32)
        if dx in started:
            acc[dx] = acc[dx] + part
        else:
            started.add(dx)
            acc[dx] = part

    def chunk(dx, k):
        return wb.at[(x + dx + NX) % NX, (y - k + NY) % NY]

    def wx_send(k):
        go(remote(chunk(0, k), chunk(0, k), wx_s.at[0, k], wx_r.at[0, k], at(dx=1)))
        go(remote(chunk(0, k), chunk(0, k), wx_s.at[1, k], wx_r.at[1, k], at(dx=-1)))

    def wx_arrived(k):
        d = chunk(-1, k)
        remote(d, d, wx_s.at[0, k], wx_r.at[0, k], at(dx=-1)).wait_recv()
        if k in (0, 1):
            go(remote(d, d, wf_s.at[k], wf_r.at[k], at(dx=1)))
        d = chunk(1, k)
        remote(d, d, wx_s.at[1, k], wx_r.at[1, k], at(dx=1)).wait_recv()
        if k in (2, 3):
            go(remote(d, d, wf_s.at[k], wf_r.at[k], at(dx=-1)))
        project(3, k)
        project(1, k)

    def wf_arrived(k):
        d = chunk(2, k)
        remote(d, d, wf_s.at[k], wf_r.at[k], at(dx=-1 if k in (0, 1) else 1)).wait_recv()
        project(2, k)

    def wy_arrived(k):
        d = chunk(0, k)
        remote(d, d, wy_s.at[k], wy_r.at[k], at(dy=-k)).wait_recv()
        wx_send(k)
        project(0, k)

    loads[1].wait()
    ones[:, HD:] = jnp.ones((QLEN, HD), jnp.bfloat16)
    token = lax.broadcasted_iota(jnp.int32, (HPB * QLEN, QLEN), 0) % QLEN
    seen = lax.broadcasted_iota(jnp.int32, (HPB * QLEN, QLEN), 1) <= token
    place = lax.broadcasted_iota(jnp.int32, (QLEN, HD), 1)

    def attend_own(n, h):
        query(n, h).wait()
        rows = slice(n * QLEN, (n + 1) * QLEN)
        key = own_ref[rows, h * HD : (h + 1) * HD]
        ones[:, :HD] = own_ref[rows, (KVH + h) * HD : (KVH + h + 1) * HD]
        packed = jnp.zeros((QLEN, HD), jnp.float32)
        for b in range(GROUPED // HPB):
            cols = [h * WIDTH + (b * HPB + i) * HD for i in range(HPB)]
            q = jnp.concatenate([queries[rows, a : a + HD] for a in cols], axis=0)
            s = lax.dot_general(q, key, (((1,), (1,)), ((), ())), preferred_element_type=jnp.float32)
            s = jnp.where(seen, s, -jnp.inf)
            peak = jnp.max(s, axis=1, keepdims=True)
            p = jnp.exp2((s - peak) * FACTOR).astype(jnp.bfloat16)
            o = jnp.dot(p, ones[...], preferred_element_type=jnp.float32)
            total = o[:, HD:]
            o = (o[:, :HD] / total).astype(jnp.bfloat16)
            score = peak + jnp.log2(total) / FACTOR
            for i, a in enumerate(cols):
                part[rows, a : a + HD] = o[i * QLEN : (i + 1) * QLEN]
                packed = jnp.where(place == b * HPB + i, score[i * QLEN : (i + 1) * QLEN], packed)
        lse[n, h] = packed
        block = (pl.ds(n * QLEN, QLEN), pl.ds(h * WIDTH, WIDTH))
        for copy in (
            pltpu.make_async_copy(part.at[block], part_ref.at[block], part_sem.at[n, h]),
            pltpu.make_async_copy(lse.at[n, h], lse_ref.at[n, h], lse_sem.at[n, h]),
        ):
            copy.start()
            local.append(copy)

    for k in range(1, NY):
        remote(info.at[k], info.at[k], in_s.at[k], in_r.at[k], at(dy=-k)).wait_recv()
    own_block.wait()
    select(0)

    own_w.wait()
    for k in range(1, NZ):
        d = wb.at[x, y, pl.ds(pl.multiple_of(zz(-k) * 128, 128), 128)]
        remote(d, d, wz_s.at[k], wz_r.at[k], at(dz=-k)).wait_recv()
    wx_send(0)
    for k in range(1, NY):
        go(remote(chunk(0, 0), chunk(0, 0), wy_s.at[k], wy_r.at[k], at(dy=k)))
    remote(hn.at[:, mine], hn.at[:, theirs], hx_s, hx_r, at(dc=1)).wait_recv()
    project(0, 0)

    attend_own(0, 0)
    z_arrived(0)
    wx_arrived(0)
    attend_own(0, 1)
    wy_arrived(1)
    wy_arrived(3)
    z_arrived(1)
    select(7)
    select(1)
    wy_arrived(2)
    wf_arrived(0)
    attend_own(0, 2)
    z_arrived(2)
    attend_own(0, 3)
    wx_arrived(1)
    z_arrived(3)
    select(6)
    select(2)
    attend_own(1, 0)
    wx_arrived(3)
    attend_own(1, 1)
    z_arrived(4)
    wx_arrived(2)
    attend_own(1, 2)
    wf_arrived(1)
    wf_arrived(3)
    attend_own(1, 3)
    z_arrived(5)
    select(5)
    select(3)
    wf_arrived(2)

    for dx in range(NX):
        xi = (x + dx) % NX
        recst[dx] = acc[dx].astype(jnp.bfloat16)
        dst = rec_ref.at[2 * xi + c]
        go(remote(recst.at[dx, theirs], dst, rx_s.at[dx], rx_r.at[dx], at(dc=1)))
        own = pltpu.make_async_copy(recst.at[dx, mine], dst, local_sem.at[12 + dx])
        own.start()
        local.append(own)

    z_arrived(6)
    select(4)

    for k in range(1, NY):
        for d in range(NZ):
            slot = slots_ref.at[((y + k) % NY) * NZ + zz(d)]
            remote(stage.at[k, d], slot, ys_s.at[k, d], ys_r.at[k, d], at(dy=k)).wait_recv()
    for dx in range(NX):
        dst = rec_ref.at[2 * ((x + dx) % NX) + (c + 1) % 2]
        remote(recst.at[dx, theirs], dst, rx_s.at[dx], rx_r.at[dx], at(dc=1)).wait_recv()
    for copy in local:
        copy.wait()
    for copy in sends:
        copy.wait_send()


def attend_kernel(ret_ref, q_ref, part_ref, lse_ref, slots_hbm, rec_hbm, out_ref, ctx, vals, sem):
    n, h = pl.program_id(0), pl.program_id(1)
    cached = TOPP * KEPT

    def fetch(i):
        copies = [
            pltpu.make_async_copy(
                slots_hbm.at[ret_ref[i, j] // 4], ctx.at[i, pl.ds(j * KEPT, KEPT)], sem.at[i, j]
            )
            for j in range(TOPP)
        ]
        return copies + [
            pltpu.make_async_copy(
                rec_hbm.at[e, pl.ds(i * QLEN, QLEN)],
                ctx.at[i, pl.ds(cached, QLEN), pl.ds(e * HD, HD)],
                sem.at[i, TOPP + e],
            )
            for e in range(2 * KVH)
        ]

    for i in range(2):

        @pl.when((n == 0) & (h == 0))
        def _():
            for copy in fetch(i):
                copy.start()

    for i in range(2):

        @pl.when((n == i) & (h == 0))
        def _():
            for copy in fetch(i):
                copy.wait()
            vals[:, HD:] = jnp.ones((TOPP * PLEN, HD), jnp.bfloat16)

    key = ctx[n, :, pl.ds(pl.multiple_of(h * HD, HD), HD)]
    vals[:, :HD] = ctx[n, :, pl.ds(pl.multiple_of((KVH + h) * HD, HD), HD)]
    for b in range(GROUPED // HPB):
        heads = [b * HPB + i for i in range(HPB)]
        q = jnp.concatenate([q_ref[:, i * HD : (i + 1) * HD] for i in heads], axis=0)
        own = jnp.concatenate([lse_ref[0, 0, :, i : i + 1] for i in heads], axis=0)
        s = lax.dot_general(q, key, (((1,), (1,)), ((), ())), preferred_element_type=jnp.float32)
        peak = jnp.maximum(jnp.max(s, axis=1, keepdims=True), own)
        p = jnp.exp2((s - peak) * FACTOR).astype(jnp.bfloat16)
        weight = jnp.exp2((own - peak) * FACTOR)
        o = jnp.dot(p, vals[...], preferred_element_type=jnp.float32)
        for i, hd in enumerate(heads):
            rows, cols = slice(i * QLEN, (i + 1) * QLEN), slice(hd * HD, (hd + 1) * HD)
            w = weight[rows]
            top = o[rows, :HD] + w * part_ref[:, cols].astype(jnp.float32)
            out_ref[:, cols] = (top / (o[rows, HD:] + w)).astype(jnp.bfloat16)


def communicate(retrieval, cache, hidden, w_kv, positions, q, own):
    dma, bf, f32 = pltpu.SemaphoreType.DMA, jnp.bfloat16, jnp.float32
    hbm = pl.BlockSpec(memory_space=pltpu.HBM)
    return pl.pallas_call(
        comm_kernel,
        out_shape=(
            jax.ShapeDtypeStruct((NY * NZ, KEPT, 1024), bf),
            jax.ShapeDtypeStruct((8, 256, 128), bf),
            jax.ShapeDtypeStruct(q.shape, bf),
            jax.ShapeDtypeStruct((2, KVH, QLEN, HD), f32),
        ),
        in_specs=[pl.BlockSpec(memory_space=pltpu.SMEM)] + [hbm] * 6,
        out_specs=(hbm,) * 4,
        scratch_shapes=[
            pltpu.VMEM((NZ, 2, 128, 1024), bf),
            pltpu.VMEM((NX, NY, 1024, 128), bf),
            pltpu.VMEM((4, 512, 1024), bf),
            pltpu.VMEM((NX, 512, 128), f32),
            pltpu.VMEM((NY, NZ, KEPT, 1024), bf),
            pltpu.VMEM((NX, 512, 128), bf),
            pltpu.VMEM((NY, 16, 512), f32),
            pltpu.VMEM(hidden.shape, bf),
            pltpu.VMEM(positions.shape, jnp.int32),
            pltpu.VMEM(q.shape, bf),
            pltpu.VMEM(own.shape, bf),
            pltpu.VMEM((QLEN, 2 * HD), bf),
            pltpu.VMEM(q.shape, bf),
            pltpu.VMEM((2, KVH, QLEN, HD), f32),
            dma((16,)), dma((3,)), dma((2, KVH)), dma((2, KVH)), dma((2, KVH)),
            dma((NZ,)), dma((NZ,)), dma((NY,)), dma((NY,)),
            dma((2, NY)), dma((2, NY)), dma((NY,)), dma((NY,)),
            dma((NY,)), dma((NY,)), dma((7,)), dma((7,)), dma((7,)), dma((7,)),
            dma((NY, NZ)), dma((NY, NZ)), dma, dma, dma((NX,)), dma((NX,)),
        ],
        compiler_params=pltpu.CompilerParams(
            collective_id=0, has_side_effects=True, vmem_limit_bytes=56 << 20
        ),
        name="exchange",
    )(retrieval, cache, hidden, w_kv, positions, q, own)


def attend(retrieval, q, part, lse, slots, rec):
    hbm = pl.BlockSpec(memory_space=pltpu.HBM)
    wide = pl.BlockSpec((QLEN, WIDTH), lambda n, h, s: (n, h))
    return pl.pallas_call(
        attend_kernel,
        out_shape=jax.ShapeDtypeStruct(q.shape, q.dtype),
        grid_spec=pltpu.PrefetchScalarGridSpec(
            num_scalar_prefetch=1,
            grid=(2, KVH),
            in_specs=[
                wide,
                wide,
                pl.BlockSpec((1, 1, QLEN, HD), lambda n, h, s: (n, h, 0, 0)),
                hbm,
                hbm,
            ],
            out_specs=wide,
            scratch_shapes=[
                pltpu.VMEM((2, TOPP * PLEN, 1024), jnp.bfloat16),
                pltpu.VMEM((TOPP * PLEN, 2 * HD), jnp.bfloat16),
                pltpu.SemaphoreType.DMA((2, 16)),
            ],
        ),
        compiler_params=pltpu.CompilerParams(vmem_limit_bytes=56 << 20),
        name="attend",
    )(retrieval, q, part, lse, slots, rec)


def local(q_rows, own_kv, cache, recomp_hidden, w_kv, retrieval, positions):
    slots, rec, part, lse = communicate(
        retrieval,
        cache.reshape(2, 128, 1024),
        recomp_hidden.reshape(256, D),
        w_kv,
        positions,
        q_rows,
        own_kv,
    )
    return attend(retrieval, q_rows, part, lse, slots, rec)


def solution(mesh):
    both = ("group", "member")
    placed = (
        P(both, None),
        P(both, None),
        P(both, None, None),
        P(both, None, None, None),
        P("member", "group"),
        P(both, None),
        P(both, None, None),
    )
    return jax.shard_map(
        local, mesh=mesh, in_specs=placed, out_specs=P(both, None), check_vma=False
    )
```

```python
import functools

import jax
import jax.numpy as jnp
from jax import lax
from jax.experimental import pallas as pl
from jax.experimental.pallas import tpu as pltpu
from jax.sharding import PartitionSpec as P

D = 4096
HQ = 64
KVH = 4
HD = 128
TOPP = 8
QLEN = 128
PLEN = 64
RECOMP = 16
KEPT = PLEN - RECOMP
EPSILON = 1e-06
LOG2E = 1.4426950408889634
MESH = pl.DeviceIdType.MESH
NX, NY, NZ = 4, 4, 8
HPB = 8
HPA = 4
HALF = KVH * HD
GROUPED = HQ // KVH
WIDTH = GROUPED * HD
FACTOR = LOG2E / HD**0.5


def comm_kernel(
    ret_ref, cache_ref, hid_hbm, w_ref, pos_hbm, q_hbm, own_hbm,
    slots_ref, rec_ref, part_ref, lse_ref,
    blk, wb, hn, acc, stage, recst, info, picks, hid_ref, pos_ref, queries, own_ref, ones, part, lse,
    local_sem, in_sem, q_sem, part_sem, lse_sem, keep_sem, wz_s, wz_r, wy_s, wy_r, wx_s, wx_r, wf_s, wf_r,
    in_s, in_r, zr_s, zr_r, zl_s, zl_r, ys_s, ys_r, hx_s, hx_r, rx_s, rx_r,
):
    g, m = lax.axis_index("group"), lax.axis_index("member")
    x, c, y, z = g // 2, g % 2, m // NZ, m % NZ

    def at(dx=0, dc=0, dy=0, dz=0):
        gg = ((x + dx + NX) % NX) * 2 + (c + dc) % 2
        return gg, ((y + dy + NY) % NY) * NZ + (z + dz + NZ) % NZ

    def remote(src, dst, s, r, dev):
        return pltpu.make_async_remote_copy(
            src_ref=src, dst_ref=dst, send_sem=s, recv_sem=r, device_id=dev, device_id_type=MESH
        )

    sends = []

    def go(copy):
        copy.start()
        sends.append(copy)
        return copy

    loads = [
        pltpu.make_async_copy(src, dst, in_sem.at[i])
        for i, (src, dst) in enumerate(((pos_hbm, pos_ref), (own_hbm, own_ref), (hid_hbm, hid_ref)))
    ]

    def query(n, h):
        block = (pl.ds(n * QLEN, QLEN), pl.ds(h * WIDTH, WIDTH))
        return pltpu.make_async_copy(q_hbm.at[block], queries.at[block], q_sem.at[n, h])

    peers = [at(dz=k) for k in range(1, NZ)] + [at(dy=k) for k in range(1, NY)]
    peers += [at(dx=1), at(dx=-1), at(dc=1)]
    barrier = pltpu.get_barrier_semaphore()
    for dev in peers:
        pl.semaphore_signal(barrier, inc=1, device_id=dev, device_id_type=MESH)

    for copy in loads:
        copy.start()
    for n in range(2):
        for h in range(KVH):
            query(n, h).start()

    lane = lax.broadcasted_iota(jnp.int32, (16, 256), 1)
    row = lane % PLEN
    loads[0].wait()
    spots = pos_ref[...].reshape(16, RECOMP)
    covered = row == spots[:, 0:1]
    for j in range(1, RECOMP):
        covered = covered | (row == spots[:, j : j + 1])
    free = jnp.where(covered[:, :PLEN], 0.0, 1.0).astype(jnp.bfloat16)
    below = lax.broadcasted_iota(jnp.int32, (PLEN, 256), 0)
    before = below < lax.broadcasted_iota(jnp.int32, (PLEN, 256), 1) % PLEN
    rank = jnp.dot(
        free, jnp.where(before, 1.0, 0.0).astype(jnp.bfloat16), preferred_element_type=jnp.float32
    )
    request = lax.broadcasted_iota(jnp.int32, (16, 256), 0)
    wanted = jnp.zeros((16, 256), jnp.int32)
    for k in range(16):
        wanted = jnp.where(request == k, ret_ref[k // TOPP, k % TOPP], wanted)
    keep = jnp.logical_not(covered) & (lane // PLEN == wanted % 4)
    info[0, :, 0:256] = jnp.where(keep, rank, -1.0)
    info[0, :, 256:512] = (wanted // 4).astype(jnp.float32)

    pl.semaphore_wait(barrier, len(peers))

    zrow = pl.multiple_of(z * 128, 128)
    for k in range(1, NZ):
        go(remote(w_ref, wb.at[x, y, pl.ds(zrow, 128)], wz_s.at[k], wz_r.at[k], at(dz=k)))
    for k in range(1, NY):
        go(remote(info.at[0], info.at[k], in_s.at[k], in_r.at[k], at(dy=k)))

    def half_right(i):
        return 0 if i == 6 else i % 2

    def half_left(i):
        return 1 if i == 6 else 1 - i % 2

    def zz(d):
        return (z + d + NZ) % NZ

    def own_half(h):
        return cache_ref.at[:, pl.ds(h * HALF, HALF)]

    def right(i):
        h = half_right(i)
        dst = blk.at[zz(-(i // 2)), h]
        return remote(own_half(h) if i < 2 else dst, dst, zr_s.at[i], zr_r.at[i], at(dz=1))

    def left(i):
        h = half_left(i)
        dst = blk.at[zz(i // 2), h]
        return remote(own_half(h) if i < 2 else dst, dst, zl_s.at[i], zl_r.at[i], at(dz=-1))

    def z_arrived(i):
        d = blk.at[zz(-1 - i // 2), half_right(i)]
        remote(d, d, zr_s.at[i], zr_r.at[i], at(dz=-1)).wait_recv()
        if i + 2 <= 6:
            go(right(i + 2))
        d = blk.at[zz(1 + i // 2), half_left(i)]
        remote(d, d, zl_s.at[i], zl_r.at[i], at(dz=1)).wait_recv()
        if i + 2 <= 6:
            go(left(i + 2))
        select(-1 - i // 2, half_right(i))
        select(1 + i // 2, half_left(i))

    own_w = pltpu.make_async_copy(w_ref, wb.at[x, y, pl.ds(zrow, 128)], local_sem.at[1])
    own_w.start()
    own_block = [
        pltpu.make_async_copy(own_half(h), blk.at[z, h], local_sem.at[2 + h]) for h in range(2)
    ]
    for copy in own_block:
        copy.start()

    loads[2].wait()
    def norm(i, carry):
        rows = pl.ds(pl.multiple_of(i * 32, 32), 32)
        h = hid_ref[rows, :].astype(jnp.float32)
        inv = lax.rsqrt(jnp.mean(h * h, axis=1, keepdims=True) + EPSILON)
        n = (h * inv).astype(jnp.bfloat16)
        for b in range(4):
            hn[b, rows, :] = n[:, b * 1024 : (b + 1) * 1024]
        return carry

    lax.fori_loop(0, 8, norm, 0)
    mine, theirs = pl.ds(0, 256), pl.ds(256, 256)
    go(remote(hn.at[:, mine], hn.at[:, theirs], hx_s, hx_r, at(dc=1)))

    for i in range(2):
        go(right(i))
        go(left(i))

    local = []

    def choose(d):
        name = (y * NZ + zz(d)).astype(jnp.float32)
        want = lax.broadcasted_iota(jnp.int32, (KEPT, 256), 0).astype(jnp.float32)
        for k in range(NY):
            hit = info[k, :, 256:512] == name
            v = jnp.max(jnp.where(hit, info[k, :, 0:256], -1.0), axis=0, keepdims=True)
            picks[d % NZ, k * KEPT : (k + 1) * KEPT] = jnp.where(want == v, 1.0, 0.0).astype(
                jnp.bfloat16
            )

    def select(d, h):
        holder, e = zz(d), d % NZ
        got = jnp.dot(picks[e], blk[holder, h], preferred_element_type=jnp.float32)
        got = got.astype(jnp.bfloat16)
        for k in range(NY):
            stage[k, e, h] = got[k * KEPT : (k + 1) * KEPT]
        slot = slots_ref.at[y * NZ + holder, h]
        for k in range(1, NY):
            go(remote(stage.at[k, e, h], slot, ys_s.at[k, e, h], ys_r.at[k, e, h], at(dy=-k)))
        kept = pltpu.make_async_copy(stage.at[0, e, h], slot, keep_sem.at[e, h])
        kept.start()
        local.append(kept)

    started = set()

    def project(dx, k):
        xi, yi = (x + dx + NX) % NX, (y - k + NY) % NY
        part = jnp.dot(hn[yi], wb[xi, yi], preferred_element_type=jnp.float32)
        if dx in started:
            acc[dx] = acc[dx] + part
        else:
            started.add(dx)
            acc[dx] = part

    def chunk(dx, k):
        return wb.at[(x + dx + NX) % NX, (y - k + NY) % NY]

    def wx_send(k):
        go(remote(chunk(0, k), chunk(0, k), wx_s.at[0, k], wx_r.at[0, k], at(dx=1)))
        go(remote(chunk(0, k), chunk(0, k), wx_s.at[1, k], wx_r.at[1, k], at(dx=-1)))

    def wx_arrived(k):
        d = chunk(-1, k)
        remote(d, d, wx_s.at[0, k], wx_r.at[0, k], at(dx=-1)).wait_recv()
        if k in (0, 1):
            go(remote(d, d, wf_s.at[k], wf_r.at[k], at(dx=1)))
        d = chunk(1, k)
        remote(d, d, wx_s.at[1, k], wx_r.at[1, k], at(dx=1)).wait_recv()
        if k in (2, 3):
            go(remote(d, d, wf_s.at[k], wf_r.at[k], at(dx=-1)))
        project(3, k)
        project(1, k)

    def wf_arrived(k):
        d = chunk(2, k)
        remote(d, d, wf_s.at[k], wf_r.at[k], at(dx=-1 if k in (0, 1) else 1)).wait_recv()
        project(2, k)

    def wy_arrived(k):
        d = chunk(0, k)
        remote(d, d, wy_s.at[k], wy_r.at[k], at(dy=-k)).wait_recv()
        wx_send(k)
        project(0, k)

    loads[1].wait()
    ones[:, HD:] = jnp.ones((QLEN, HD), jnp.bfloat16)
    token = lax.broadcasted_iota(jnp.int32, (HPB * QLEN, QLEN), 0) % QLEN
    seen = lax.broadcasted_iota(jnp.int32, (HPB * QLEN, QLEN), 1) <= token

    def attend_own(n, h):
        query(n, h).wait()
        rows = slice(n * QLEN, (n + 1) * QLEN)
        key = own_ref[rows, h * HD : (h + 1) * HD]
        ones[:, :HD] = own_ref[rows, (KVH + h) * HD : (KVH + h + 1) * HD]
        for b in range(GROUPED // HPB):
            cols = [h * WIDTH + (b * HPB + i) * HD for i in range(HPB)]
            q = jnp.concatenate([queries[rows, a : a + HD] for a in cols], axis=0)
            s = lax.dot_general(q, key, (((1,), (1,)), ((), ())), preferred_element_type=jnp.float32)
            s = jnp.where(seen, s, -jnp.inf)
            peak = jnp.max(s, axis=1, keepdims=True)
            p = jnp.exp2((s - peak) * FACTOR).astype(jnp.bfloat16)
            o = jnp.dot(p, ones[...], preferred_element_type=jnp.float32)
            total = o[:, HD:]
            o = (o[:, :HD] / total).astype(jnp.bfloat16)
            score = peak + jnp.log2(total) / FACTOR
            for i, a in enumerate(cols):
                part[rows, a : a + HD] = o[i * QLEN : (i + 1) * QLEN]
                lse[rows, a : a + HD] = score[i * QLEN : (i + 1) * QLEN]
        block = (pl.ds(n * QLEN, QLEN), pl.ds(h * WIDTH, WIDTH))
        for copy in (
            pltpu.make_async_copy(part.at[block], part_ref.at[block], part_sem.at[n, h]),
            pltpu.make_async_copy(lse.at[block], lse_ref.at[block], lse_sem.at[n, h]),
        ):
            copy.start()
            local.append(copy)

    for k in range(1, NY):
        remote(info.at[k], info.at[k], in_s.at[k], in_r.at[k], at(dy=-k)).wait_recv()
    for d in range(NZ):
        choose(d)
    for copy in own_block:
        copy.wait()
    select(0, 0)
    select(0, 1)
    attend_own(0, 0)

    own_w.wait()
    for k in range(1, NZ):
        d = wb.at[x, y, pl.ds(pl.multiple_of(zz(-k) * 128, 128), 128)]
        remote(d, d, wz_s.at[k], wz_r.at[k], at(dz=-k)).wait_recv()
    wx_send(0)
    for k in (1, 3):
        go(remote(chunk(0, 0), chunk(0, 0), wy_s.at[k], wy_r.at[k], at(dy=k)))
    remote(hn.at[:, mine], hn.at[:, theirs], hx_s, hx_r, at(dc=1)).wait_recv()
    project(0, 0)
    attend_own(0, 1)
    z_arrived(0)
    wx_arrived(0)
    wy_arrived(1)
    wy_arrived(3)
    go(remote(chunk(0, 0), chunk(0, 0), wy_s.at[2], wy_r.at[2], at(dy=2)))
    attend_own(0, 2)
    z_arrived(1)
    attend_own(0, 3)
    wf_arrived(0)
    wy_arrived(2)
    z_arrived(2)
    attend_own(1, 0)
    wx_arrived(1)
    attend_own(1, 1)
    z_arrived(3)
    attend_own(1, 2)
    wx_arrived(3)
    attend_own(1, 3)
    z_arrived(4)
    wx_arrived(2)
    wf_arrived(1)
    wf_arrived(3)
    z_arrived(5)
    wf_arrived(2)

    for dx in range(NX):
        xi = (x + dx) % NX
        recst[dx] = acc[dx].astype(jnp.bfloat16)
        dst = rec_ref.at[2 * xi + c]
        go(remote(recst.at[dx, theirs], dst, rx_s.at[dx], rx_r.at[dx], at(dc=1)))
        own = pltpu.make_async_copy(recst.at[dx, mine], dst, local_sem.at[12 + dx])
        own.start()
        local.append(own)

    z_arrived(6)

    for k in range(1, NY):
        for d in range(NZ):
            for h in range(2):
                slot = slots_ref.at[((y + k) % NY) * NZ + zz(d), h]
                src = stage.at[k, d, h]
                remote(src, slot, ys_s.at[k, d, h], ys_r.at[k, d, h], at(dy=k)).wait_recv()
    for dx in range(NX):
        dst = rec_ref.at[2 * ((x + dx) % NX) + (c + 1) % 2]
        remote(recst.at[dx, theirs], dst, rx_s.at[dx], rx_r.at[dx], at(dc=1)).wait_recv()
    for copy in local:
        copy.wait()
    for copy in sends:
        copy.wait_send()


def attend_kernel(
    ret_ref, q_hbm, part_hbm, lse_hbm, slots_hbm, rec_hbm, out_hbm,
    ctx, vals, queries, part, lse, out, sem, q_sem, part_sem, lse_sem, out_sem,
):
    cached, steps = TOPP * KEPT, 2 * KVH

    def fetch(i):
        copies = [
            pltpu.make_async_copy(
                slots_hbm.at[ret_ref[i, j] // 4], ctx.at[i, :, pl.ds(j * KEPT, KEPT)], sem.at[i, j]
            )
            for j in range(TOPP)
        ]
        return copies + [
            pltpu.make_async_copy(
                rec_hbm.at[e, pl.ds(i * QLEN, QLEN)],
                ctx.at[i, e // KVH, pl.ds(cached, QLEN), pl.ds(e % KVH * HD, HD)],
                sem.at[i, TOPP + e],
            )
            for e in range(2 * KVH)
        ]

    def block(t):
        row = pl.multiple_of(t // KVH * QLEN, QLEN)
        col = pl.multiple_of(t % KVH * WIDTH, WIDTH)
        return pl.ds(row, QLEN), pl.ds(col, WIDTH)

    def inputs(t):
        return [
            pltpu.make_async_copy(src.at[block(t)], dst.at[block(t)], s.at[t])
            for src, dst, s in (
                (q_hbm, queries, q_sem), (part_hbm, part, part_sem), (lse_hbm, lse, lse_sem),
            )
        ]

    def output(t):
        return pltpu.make_async_copy(out.at[block(t)], out_hbm.at[block(t)], out_sem.at[t])

    for copy in fetch(0) + inputs(0) + inputs(1):
        copy.start()
    vals[:, HD:] = jnp.ones((TOPP * PLEN, HD), jnp.bfloat16)
    for copy in fetch(0):
        copy.wait()

    def step(t, carry):
        for copy in inputs(t):
            copy.wait()

        @pl.when(t < steps - 2)
        def _():
            for copy in inputs(t + 2):
                copy.start()

        @pl.when(t == 1)
        def _():
            for copy in fetch(1):
                copy.start()

        @pl.when(t == KVH)
        def _():
            for copy in fetch(1):
                copy.wait()

        n, h = t // KVH, t % KVH
        rows = pl.ds(pl.multiple_of(n * QLEN, QLEN), QLEN)
        head = pl.ds(pl.multiple_of(h * HD, HD), HD)
        key = ctx[n, 0, :, head]
        vals[:, :HD] = ctx[n, 1, :, head]

        def cols(b, i):
            return pl.ds(pl.multiple_of(h * WIDTH + (b * HPA + i) * HD, HD), HD)

        def stack(ref, b):
            return jnp.concatenate([ref[rows, cols(b, i)] for i in range(HPA)], axis=0)

        def score(b):
            return lax.dot_general(
                stack(queries, b), key, (((1,), (1,)), ((), ())), preferred_element_type=jnp.float32
            )

        def finish(b, s):
            own = stack(lse, b)
            peak = jnp.maximum(jnp.max(s, axis=1, keepdims=True), own)
            p = jnp.concatenate(
                [
                    jnp.exp2((s[:, c : c + HD] - peak) * FACTOR).astype(jnp.bfloat16)
                    for c in range(0, TOPP * PLEN, HD)
                ],
                axis=1,
            )
            weight = jnp.exp2((own - peak) * FACTOR)
            o = jnp.dot(p, vals[...], preferred_element_type=jnp.float32)
            top = o[:, :HD] + weight * stack(part, b).astype(jnp.float32)
            o = (top / (o[:, HD:] + weight)).astype(jnp.bfloat16)
            for i in range(HPA):
                out[rows, cols(b, i)] = o[i * QLEN : (i + 1) * QLEN]

        groups = GROUPED // HPA
        s = score(0)
        for b in range(groups):
            later = score(b + 1) if b + 1 < groups else None
            finish(b, s)
            s = later
        output(t).start()
        return carry

    lax.fori_loop(0, steps, step, 0)
    for t in range(steps):
        output(t).wait()


def communicate(retrieval, cache, hidden, w_kv, positions, q, own):
    dma, bf, f32 = pltpu.SemaphoreType.DMA, jnp.bfloat16, jnp.float32
    hbm = pl.BlockSpec(memory_space=pltpu.HBM)
    return pl.pallas_call(
        comm_kernel,
        out_shape=(
            jax.ShapeDtypeStruct((NY * NZ, 2, KEPT, HALF), bf),
            jax.ShapeDtypeStruct((8, 256, 128), bf),
            jax.ShapeDtypeStruct(q.shape, bf),
            jax.ShapeDtypeStruct(q.shape, f32),
        ),
        in_specs=[pl.BlockSpec(memory_space=pltpu.SMEM)] + [hbm] * 6,
        out_specs=(hbm,) * 4,
        scratch_shapes=[
            pltpu.VMEM((NZ, 2, 256, HALF), bf),
            pltpu.VMEM((NX, NY, 1024, 128), bf),
            pltpu.VMEM((4, 512, 1024), bf),
            pltpu.VMEM((NX, 512, 128), f32),
            pltpu.VMEM((NY, NZ, 2, KEPT, HALF), bf),
            pltpu.VMEM((NX, 512, 128), bf),
            pltpu.VMEM((NY, 16, 512), f32),
            pltpu.VMEM((NZ, NY * KEPT, 256), bf),
            pltpu.VMEM(hidden.shape, bf),
            pltpu.VMEM(positions.shape, jnp.int32),
            pltpu.VMEM(q.shape, bf),
            pltpu.VMEM(own.shape, bf),
            pltpu.VMEM((QLEN, 2 * HD), bf),
            pltpu.VMEM(q.shape, bf),
            pltpu.VMEM(q.shape, f32),
            dma((16,)), dma((3,)), dma((2, KVH)), dma((2, KVH)), dma((2, KVH)), dma((NZ, 2)),
            dma((NZ,)), dma((NZ,)), dma((NY,)), dma((NY,)),
            dma((2, NY)), dma((2, NY)), dma((NY,)), dma((NY,)),
            dma((NY,)), dma((NY,)), dma((7,)), dma((7,)), dma((7,)), dma((7,)),
            dma((NY, NZ, 2)), dma((NY, NZ, 2)), dma, dma, dma((NX,)), dma((NX,)),
        ],
        compiler_params=pltpu.CompilerParams(
            collective_id=0, has_side_effects=True, vmem_limit_bytes=56 << 20
        ),
        name="exchange",
    )(retrieval, cache, hidden, w_kv, positions, q, own)


def attend(retrieval, q, part, lse, slots, rec):
    dma, bf = pltpu.SemaphoreType.DMA, jnp.bfloat16
    hbm = pl.BlockSpec(memory_space=pltpu.HBM)
    return pl.pallas_call(
        attend_kernel,
        out_shape=jax.ShapeDtypeStruct(q.shape, q.dtype),
        in_specs=[pl.BlockSpec(memory_space=pltpu.SMEM)] + [hbm] * 5,
        out_specs=hbm,
        scratch_shapes=[
            pltpu.VMEM((2, 2, TOPP * PLEN, HALF), bf),
            pltpu.VMEM((TOPP * PLEN, 2 * HD), bf),
            pltpu.VMEM(q.shape, bf),
            pltpu.VMEM(q.shape, bf),
            pltpu.VMEM(q.shape, jnp.float32),
            pltpu.VMEM(q.shape, bf),
            dma((2, TOPP + 2 * KVH)), dma((8,)), dma((8,)), dma((8,)), dma((8,)),
        ],
        compiler_params=pltpu.CompilerParams(vmem_limit_bytes=56 << 20),
        name="attend",
    )(retrieval, q, part, lse, slots, rec)


def local(q_rows, own_kv, cache, recomp_hidden, w_kv, retrieval, positions):
    slots, rec, part, lse = communicate(
        retrieval,
        cache.reshape(256, 1024),
        recomp_hidden.reshape(256, D),
        w_kv,
        positions,
        q_rows,
        own_kv,
    )
    return attend(retrieval, q_rows, part, lse, slots, rec)


def solution(mesh):
    both = ("group", "member")
    placed = (
        P(both, None),
        P(both, None),
        P(both, None, None),
        P(both, None, None, None),
        P("member", "group"),
        P(both, None),
        P(both, None, None),
    )
    return jax.shard_map(
        local, mesh=mesh, in_specs=placed, out_specs=P(both, None), check_vma=False
    )
```

```python
import functools

import jax
import jax.numpy as jnp
from jax import lax
from jax.experimental import pallas as pl
from jax.experimental.pallas import tpu as pltpu
from jax.sharding import PartitionSpec as P

D = 4096
HQ = 64
KVH = 4
HD = 128
TOPP = 8
QLEN = 128
PLEN = 64
RECOMP = 16
KEPT = PLEN - RECOMP
EPSILON = 1e-06
LOG2E = 1.4426950408889634
MESH = pl.DeviceIdType.MESH
NX, NY, NZ = 4, 4, 8
HPB = 8
HPA = 4
PARTS = 4
PART = 2 * KVH * HD // PARTS
GROUPED = HQ // KVH
WIDTH = GROUPED * HD
FACTOR = LOG2E / HD**0.5


def comm_kernel(
    ret_ref, cache_ref, hid_hbm, w_ref, pos_hbm, q_hbm, own_hbm,
    slots_ref, rec_ref, part_ref, lse_ref,
    blk, wb, hn, acc, stage, recst, info, picks, hid_ref, pos_ref, queries, own_ref, ones, part, lse,
    local_sem, in_sem, q_sem, part_sem, lse_sem, keep_sem, wz_s, wz_r, wy_s, wy_r, wx_s, wx_r, wf_s, wf_r,
    in_s, in_r, zr_s, zr_r, zl_s, zl_r, ys_s, ys_r, hx_s, hx_r, rx_s, rx_r,
):
    g, m = lax.axis_index("group"), lax.axis_index("member")
    x, c, y, z = g // 2, g % 2, m // NZ, m % NZ

    def at(dx=0, dc=0, dy=0, dz=0):
        gg = ((x + dx + NX) % NX) * 2 + (c + dc) % 2
        return gg, ((y + dy + NY) % NY) * NZ + (z + dz + NZ) % NZ

    def remote(src, dst, s, r, dev):
        return pltpu.make_async_remote_copy(
            src_ref=src, dst_ref=dst, send_sem=s, recv_sem=r, device_id=dev, device_id_type=MESH
        )

    sends = []

    def go(copy):
        copy.start()
        sends.append(copy)
        return copy

    loads = [
        pltpu.make_async_copy(src, dst, in_sem.at[i])
        for i, (src, dst) in enumerate(((pos_hbm, pos_ref), (own_hbm, own_ref), (hid_hbm, hid_ref)))
    ]

    def query(n, h):
        block = (pl.ds(n * QLEN, QLEN), pl.ds(h * WIDTH, WIDTH))
        return pltpu.make_async_copy(q_hbm.at[block], queries.at[block], q_sem.at[n, h])

    peers = [at(dz=k) for k in (1, 2, -2, -1)] + [at(dy=k) for k in range(1, NY)]
    peers += [at(dx=1), at(dx=-1), at(dc=1)]
    barrier = pltpu.get_barrier_semaphore()
    for dev in peers:
        pl.semaphore_signal(barrier, inc=1, device_id=dev, device_id_type=MESH)

    for copy in loads:
        copy.start()
    for n in range(2):
        for h in range(KVH):
            query(n, h).start()

    lane = lax.broadcasted_iota(jnp.int32, (16, 256), 1)
    row = lane % PLEN
    loads[0].wait()
    spots = pos_ref[...].reshape(16, RECOMP)
    covered = row == spots[:, 0:1]
    for j in range(1, RECOMP):
        covered = covered | (row == spots[:, j : j + 1])
    free = jnp.where(covered[:, :PLEN], 0.0, 1.0).astype(jnp.bfloat16)
    below = lax.broadcasted_iota(jnp.int32, (PLEN, 256), 0)
    before = below < lax.broadcasted_iota(jnp.int32, (PLEN, 256), 1) % PLEN
    rank = jnp.dot(
        free, jnp.where(before, 1.0, 0.0).astype(jnp.bfloat16), preferred_element_type=jnp.float32
    )
    request = lax.broadcasted_iota(jnp.int32, (16, 256), 0)
    wanted = jnp.zeros((16, 256), jnp.int32)
    for k in range(16):
        wanted = jnp.where(request == k, ret_ref[k // TOPP, k % TOPP], wanted)
    keep = jnp.logical_not(covered) & (lane // PLEN == wanted % 4)
    info[0, :, 0:256] = jnp.where(keep, rank, -1.0)
    info[0, :, 256:512] = (wanted // 4).astype(jnp.float32)

    pl.semaphore_wait(barrier, len(peers))

    zrow = pl.multiple_of(z * 128, 128)
    for k in (1, 2, 6, 7):
        dst = wb.at[x, y, pl.ds(zrow, 128)]
        go(remote(w_ref, dst, wz_s.at[k], wz_r.at[k], at(dz=k if k < 4 else k - NZ)))
    for k in range(1, NY):
        go(remote(info.at[0], info.at[k], in_s.at[k], in_r.at[k], at(dy=k)))

    last = 3 * PARTS

    def part_right(i):
        return i % PARTS

    def part_left(i):
        return PARTS - 1 - i % PARTS

    def zz(d):
        return (z + d + NZ) % NZ

    def own_part(h):
        return cache_ref.at[:, pl.ds(h * PART, PART)]

    def right(i):
        h = part_right(i)
        dst = blk.at[zz(-(i // PARTS)), h]
        return remote(own_part(h) if i < PARTS else dst, dst, zr_s.at[i], zr_r.at[i], at(dz=1))

    def left(i):
        h = part_left(i)
        dst = blk.at[zz(i // PARTS), h]
        return remote(own_part(h) if i < PARTS else dst, dst, zl_s.at[i], zl_r.at[i], at(dz=-1))

    def z_arrived(i):
        d = blk.at[zz(-1 - i // PARTS), part_right(i)]
        remote(d, d, zr_s.at[i], zr_r.at[i], at(dz=-1)).wait_recv()
        if i + PARTS < last + PARTS // 2:
            go(right(i + PARTS))
        d = blk.at[zz(1 + i // PARTS), part_left(i)]
        remote(d, d, zl_s.at[i], zl_r.at[i], at(dz=1)).wait_recv()
        if i + PARTS < last + PARTS // 2:
            go(left(i + PARTS))
        select(-1 - i // PARTS, part_right(i))
        select(1 + i // PARTS, part_left(i))

    own_w = pltpu.make_async_copy(w_ref, wb.at[x, y, pl.ds(zrow, 128)], local_sem.at[1])
    own_w.start()
    own_block = [
        pltpu.make_async_copy(own_part(h), blk.at[z, h], local_sem.at[2 + h])
        for h in range(PARTS)
    ]
    for copy in own_block:
        copy.start()

    loads[2].wait()
    def norm(i, carry):
        rows = pl.ds(pl.multiple_of(i * 32, 32), 32)
        h = hid_ref[rows, :].astype(jnp.float32)
        inv = lax.rsqrt(jnp.mean(h * h, axis=1, keepdims=True) + EPSILON)
        n = (h * inv).astype(jnp.bfloat16)
        for b in range(4):
            hn[b, rows, :] = n[:, b * 1024 : (b + 1) * 1024]
        return carry

    lax.fori_loop(0, 8, norm, 0)
    mine, theirs = pl.ds(0, 256), pl.ds(256, 256)
    go(remote(hn.at[:, mine], hn.at[:, theirs], hx_s, hx_r, at(dc=1)))

    for i in range(PARTS):
        go(right(i))
        go(left(i))

    def w_row(k):
        return wb.at[x, y, pl.ds(pl.multiple_of(zz(-k) * 128, 128), 128)]

    def wz_arrived(k):
        d = w_row(k)
        remote(d, d, wz_s.at[k], wz_r.at[k], at(dz=-k if k < 4 else NZ - k)).wait_recv()

    def wz_forward(k, steps):
        j = (k + steps) % NZ
        go(remote(w_row(k), w_row(k), wz_s.at[j], wz_r.at[j], at(dz=steps)))

    wz_arrived(2)
    wz_forward(2, 1)
    wz_forward(2, 2)
    wz_arrived(6)
    wz_forward(6, -1)

    local = []

    def choose(d):
        name = (y * NZ + zz(d)).astype(jnp.float32)
        want = lax.broadcasted_iota(jnp.int32, (KEPT, 256), 0).astype(jnp.float32)
        for k in range(NY):
            hit = info[k, :, 256:512] == name
            v = jnp.max(jnp.where(hit, info[k, :, 0:256], -1.0), axis=0, keepdims=True)
            picks[d % NZ, k * KEPT : (k + 1) * KEPT] = jnp.where(want == v, 1.0, 0.0).astype(
                jnp.bfloat16
            )

    def select(d, h):
        holder, e = zz(d), d % NZ
        got = jnp.dot(picks[e], blk[holder, h], preferred_element_type=jnp.float32)
        got = got.astype(jnp.bfloat16)
        for k in range(NY):
            stage[k, e, h] = got[k * KEPT : (k + 1) * KEPT]
        slot = slots_ref.at[y * NZ + holder, h]
        for k in range(1, NY):
            remote(stage.at[k, e, h], slot, ys_s.at[k], ys_r.at[k], at(dy=-k)).start()
        pltpu.make_async_copy(stage.at[0, e, h], slot, keep_sem).start()

    started = set()

    def project(dx, k):
        xi, yi = (x + dx + NX) % NX, (y - k + NY) % NY
        part = jnp.dot(hn[yi], wb[xi, yi], preferred_element_type=jnp.float32)
        if dx in started:
            acc[dx] = acc[dx] + part
        else:
            started.add(dx)
            acc[dx] = part

    def chunk(dx, k):
        return wb.at[(x + dx + NX) % NX, (y - k + NY) % NY]

    def wx_send(k):
        go(remote(chunk(0, k), chunk(0, k), wx_s.at[0, k], wx_r.at[0, k], at(dx=1)))
        go(remote(chunk(0, k), chunk(0, k), wx_s.at[1, k], wx_r.at[1, k], at(dx=-1)))

    def wx_arrived(k):
        d = chunk(-1, k)
        remote(d, d, wx_s.at[0, k], wx_r.at[0, k], at(dx=-1)).wait_recv()
        if k in (0, 1):
            go(remote(d, d, wf_s.at[k], wf_r.at[k], at(dx=1)))
        d = chunk(1, k)
        remote(d, d, wx_s.at[1, k], wx_r.at[1, k], at(dx=1)).wait_recv()
        if k in (2, 3):
            go(remote(d, d, wf_s.at[k], wf_r.at[k], at(dx=-1)))
        project(3, k)
        project(1, k)

    def wf_arrived(k):
        d = chunk(2, k)
        remote(d, d, wf_s.at[k], wf_r.at[k], at(dx=-1 if k in (0, 1) else 1)).wait_recv()
        project(2, k)

    def wy_arrived(k):
        d = chunk(0, k)
        remote(d, d, wy_s.at[k], wy_r.at[k], at(dy=-k)).wait_recv()
        wx_send(k)
        project(0, k)

    loads[1].wait()
    ones[:, HD:] = jnp.ones((QLEN, HD), jnp.bfloat16)
    token = lax.broadcasted_iota(jnp.int32, (HPB * QLEN, QLEN), 0) % QLEN
    seen = lax.broadcasted_iota(jnp.int32, (HPB * QLEN, QLEN), 1) <= token

    def attend_own(n, h):
        query(n, h).wait()
        rows = slice(n * QLEN, (n + 1) * QLEN)
        key = own_ref[rows, h * HD : (h + 1) * HD]
        ones[:, :HD] = own_ref[rows, (KVH + h) * HD : (KVH + h + 1) * HD]
        for b in range(GROUPED // HPB):
            cols = [h * WIDTH + (b * HPB + i) * HD for i in range(HPB)]
            q = jnp.concatenate([queries[rows, a : a + HD] for a in cols], axis=0)
            s = lax.dot_general(q, key, (((1,), (1,)), ((), ())), preferred_element_type=jnp.float32)
            s = jnp.where(seen, s, -jnp.inf)
            peak = jnp.max(s, axis=1, keepdims=True)
            p = jnp.exp2((s - peak) * FACTOR).astype(jnp.bfloat16)
            o = jnp.dot(p, ones[...], preferred_element_type=jnp.float32)
            total = o[:, HD:]
            o = (o[:, :HD] / total).astype(jnp.bfloat16)
            score = peak + jnp.log2(total) / FACTOR
            for i, a in enumerate(cols):
                part[rows, a : a + HD] = o[i * QLEN : (i + 1) * QLEN]
                lse[rows, a : a + HD] = score[i * QLEN : (i + 1) * QLEN]
        block = (pl.ds(n * QLEN, QLEN), pl.ds(h * WIDTH, WIDTH))
        for copy in (
            pltpu.make_async_copy(part.at[block], part_ref.at[block], part_sem.at[n, h]),
            pltpu.make_async_copy(lse.at[block], lse_ref.at[block], lse_sem.at[n, h]),
        ):
            copy.start()
            local.append(copy)

    for k in range(1, NY):
        remote(info.at[k], info.at[k], in_s.at[k], in_r.at[k], at(dy=-k)).wait_recv()
    for d in range(NZ):
        choose(d)
    for copy in own_block:
        copy.wait()
    for h in range(PARTS):
        select(0, h)
    attend_own(0, 0)

    own_w.wait()
    for k in (1, 7, 3, 5, 4):
        wz_arrived(k)
    wx_send(0)
    for k in (1, 3):
        go(remote(chunk(0, 0), chunk(0, 0), wy_s.at[k], wy_r.at[k], at(dy=k)))
    remote(hn.at[:, mine], hn.at[:, theirs], hx_s, hx_r, at(dc=1)).wait_recv()
    project(0, 0)
    z_arrived(0)
    z_arrived(1)
    attend_own(0, 1)
    wx_arrived(0)
    wy_arrived(1)
    wy_arrived(3)
    go(remote(chunk(0, 0), chunk(0, 0), wy_s.at[2], wy_r.at[2], at(dy=2)))
    z_arrived(2)
    z_arrived(3)
    attend_own(0, 2)
    z_arrived(4)
    wf_arrived(0)
    attend_own(0, 3)
    z_arrived(5)
    wy_arrived(2)
    z_arrived(6)
    attend_own(1, 0)
    wx_arrived(1)
    z_arrived(7)
    attend_own(1, 1)
    z_arrived(8)
    wx_arrived(3)
    attend_own(1, 2)
    z_arrived(9)
    attend_own(1, 3)
    z_arrived(10)
    wx_arrived(2)
    z_arrived(11)
    wf_arrived(1)
    wf_arrived(3)
    z_arrived(12)
    wf_arrived(2)

    for dx in range(NX):
        xi = (x + dx) % NX
        recst[dx] = acc[dx].astype(jnp.bfloat16)
        dst = rec_ref.at[2 * xi + c]
        go(remote(recst.at[dx, theirs], dst, rx_s.at[dx], rx_r.at[dx], at(dc=1)))
        own = pltpu.make_async_copy(recst.at[dx, mine], dst, local_sem.at[12 + dx])
        own.start()
        local.append(own)

    z_arrived(13)

    for dx in range(NX):
        dst = rec_ref.at[2 * ((x + dx) % NX) + (c + 1) % 2]
        remote(recst.at[dx, theirs], dst, rx_s.at[dx], rx_r.at[dx], at(dc=1)).wait_recv()
    for copy in local:
        copy.wait()
    for copy in sends:
        copy.wait_send()
    pltpu.make_async_copy(stage.at[0], slots_ref.at[pl.ds(y * NZ, NZ)], keep_sem).wait()
    for k in range(1, NY):
        rows = slots_ref.at[pl.ds((y + k) % NY * NZ, NZ)]
        remote(stage.at[k], rows, ys_s.at[k], ys_r.at[k], at(dy=-k)).wait_send()
        remote(stage.at[k], rows, ys_s.at[k], ys_r.at[k], at(dy=k)).wait_recv()


def attend_kernel(
    ret_ref, q_hbm, part_hbm, lse_hbm, slots_hbm, rec_hbm, out_hbm,
    ctx, vals, queries, part, lse, out, sem, q_sem, part_sem, lse_sem, out_sem,
):
    cached, steps = TOPP * KEPT, 2 * KVH

    def fetch(i):
        copies = [
            pltpu.make_async_copy(
                slots_hbm.at[ret_ref[i, j] // 4], ctx.at[i, :, pl.ds(j * KEPT, KEPT)], sem.at[i, j]
            )
            for j in range(TOPP)
        ]
        return copies + [
            pltpu.make_async_copy(
                rec_hbm.at[e, pl.ds(i * QLEN, QLEN)],
                ctx.at[i, e // 2, pl.ds(cached, QLEN), pl.ds(e % 2 * HD, HD)],
                sem.at[i, TOPP + e],
            )
            for e in range(2 * KVH)
        ]

    def block(t):
        row = pl.multiple_of(t // KVH * QLEN, QLEN)
        col = pl.multiple_of(t % KVH * WIDTH, WIDTH)
        return pl.ds(row, QLEN), pl.ds(col, WIDTH)

    def inputs(t):
        return [
            pltpu.make_async_copy(src.at[block(t)], dst.at[block(t)], s.at[t])
            for src, dst, s in (
                (q_hbm, queries, q_sem), (part_hbm, part, part_sem), (lse_hbm, lse, lse_sem),
            )
        ]

    def output(t):
        return pltpu.make_async_copy(out.at[block(t)], out_hbm.at[block(t)], out_sem.at[t])

    for copy in fetch(0) + inputs(0):
        copy.start()
    vals[:, HD:] = jnp.ones((TOPP * PLEN, HD), jnp.bfloat16)
    for copy in fetch(0):
        copy.wait()
    for copy in inputs(1):
        copy.start()

    def step(t, carry):
        for copy in inputs(t):
            copy.wait()

        @pl.when(t < steps - 2)
        def _():
            for copy in inputs(t + 2):
                copy.start()

        @pl.when(t == 1)
        def _():
            for copy in fetch(1):
                copy.start()

        @pl.when(t == KVH)
        def _():
            for copy in fetch(1):
                copy.wait()

        n, h = t // KVH, t % KVH
        rows = pl.ds(pl.multiple_of(n * QLEN, QLEN), QLEN)
        head = pl.ds(pl.multiple_of(h % 2 * HD, HD), HD)
        key = ctx[n, h // 2, :, head]
        vals[:, :HD] = ctx[n, 2 + h // 2, :, head]

        def cols(b, i):
            return pl.ds(pl.multiple_of(h * WIDTH + (b * HPA + i) * HD, HD), HD)

        def stack(ref, b):
            return jnp.concatenate([ref[rows, cols(b, i)] for i in range(HPA)], axis=0)

        def score(b):
            return lax.dot_general(
                stack(queries, b), key, (((1,), (1,)), ((), ())), preferred_element_type=jnp.float32
            )

        def finish(b, s):
            own = stack(lse, b)
            peak = jnp.maximum(jnp.max(s, axis=1, keepdims=True), own)
            p = jnp.concatenate(
                [
                    jnp.exp2((s[:, c : c + HD] - peak) * FACTOR).astype(jnp.bfloat16)
                    for c in range(0, TOPP * PLEN, HD)
                ],
                axis=1,
            )
            weight = jnp.exp2((own - peak) * FACTOR)
            o = jnp.dot(p, vals[...], preferred_element_type=jnp.float32)
            top = o[:, :HD] + weight * stack(part, b).astype(jnp.float32)
            o = (top / (o[:, HD:] + weight)).astype(jnp.bfloat16)
            for i in range(HPA):
                out[rows, cols(b, i)] = o[i * QLEN : (i + 1) * QLEN]

        groups = GROUPED // HPA
        s = score(0)
        for b in range(groups):
            later = score(b + 1) if b + 1 < groups else None
            finish(b, s)
            s = later
        output(t).start()
        return carry

    lax.fori_loop(0, steps, step, 0)
    for t in range(steps):
        output(t).wait()


def communicate(retrieval, cache, hidden, w_kv, positions, q, own):
    dma, bf, f32 = pltpu.SemaphoreType.DMA, jnp.bfloat16, jnp.float32
    hbm = pl.BlockSpec(memory_space=pltpu.HBM)
    return pl.pallas_call(
        comm_kernel,
        out_shape=(
            jax.ShapeDtypeStruct((NY * NZ, PARTS, KEPT, PART), bf),
            jax.ShapeDtypeStruct((8, 256, 128), bf),
            jax.ShapeDtypeStruct(q.shape, bf),
            jax.ShapeDtypeStruct(q.shape, f32),
        ),
        in_specs=[pl.BlockSpec(memory_space=pltpu.SMEM)] + [hbm] * 6,
        out_specs=(hbm,) * 4,
        scratch_shapes=[
            pltpu.VMEM((NZ, PARTS, 256, PART), bf),
            pltpu.VMEM((NX, NY, 1024, 128), bf),
            pltpu.VMEM((4, 512, 1024), bf),
            pltpu.VMEM((NX, 512, 128), f32),
            pltpu.VMEM((NY, NZ, PARTS, KEPT, PART), bf),
            pltpu.VMEM((NX, 512, 128), bf),
            pltpu.VMEM((NY, 16, 512), f32),
            pltpu.VMEM((NZ, NY * KEPT, 256), bf),
            pltpu.VMEM(hidden.shape, bf),
            pltpu.VMEM(positions.shape, jnp.int32),
            pltpu.VMEM(q.shape, bf),
            pltpu.VMEM(own.shape, bf),
            pltpu.VMEM((QLEN, 2 * HD), bf),
            pltpu.VMEM(q.shape, bf),
            pltpu.VMEM(q.shape, f32),
            dma((16,)), dma((3,)), dma((2, KVH)), dma((2, KVH)), dma((2, KVH)), dma,
            dma((NZ,)), dma((NZ,)), dma((NY,)), dma((NY,)),
            dma((2, NY)), dma((2, NY)), dma((NY,)), dma((NY,)),
            dma((NY,)), dma((NY,)), dma((14,)), dma((14,)), dma((14,)), dma((14,)),
            dma((NY,)), dma((NY,)), dma, dma, dma((NX,)), dma((NX,)),
        ],
        compiler_params=pltpu.CompilerParams(
            collective_id=0, has_side_effects=True, vmem_limit_bytes=56 << 20
        ),
        name="exchange",
    )(retrieval, cache, hidden, w_kv, positions, q, own)


def attend(retrieval, q, part, lse, slots, rec):
    dma, bf = pltpu.SemaphoreType.DMA, jnp.bfloat16
    hbm = pl.BlockSpec(memory_space=pltpu.HBM)
    return pl.pallas_call(
        attend_kernel,
        out_shape=jax.ShapeDtypeStruct(q.shape, q.dtype),
        in_specs=[pl.BlockSpec(memory_space=pltpu.SMEM)] + [hbm] * 5,
        out_specs=hbm,
        scratch_shapes=[
            pltpu.VMEM((2, PARTS, TOPP * PLEN, PART), bf),
            pltpu.VMEM((TOPP * PLEN, 2 * HD), bf),
            pltpu.VMEM(q.shape, bf),
            pltpu.VMEM(q.shape, bf),
            pltpu.VMEM(q.shape, jnp.float32),
            pltpu.VMEM(q.shape, bf),
            dma((2, TOPP + 2 * KVH)), dma((8,)), dma((8,)), dma((8,)), dma((8,)),
        ],
        compiler_params=pltpu.CompilerParams(vmem_limit_bytes=56 << 20),
        name="attend",
    )(retrieval, q, part, lse, slots, rec)


def local(q_rows, own_kv, cache, recomp_hidden, w_kv, retrieval, positions):
    slots, rec, part, lse = communicate(
        retrieval,
        cache.reshape(256, 1024),
        recomp_hidden.reshape(256, D),
        w_kv,
        positions,
        q_rows,
        own_kv,
    )
    return attend(retrieval, q_rows, part, lse, slots, rec)


def solution(mesh):
    both = ("group", "member")
    placed = (
        P(both, None),
        P(both, None),
        P(both, None, None),
        P(both, None, None, None),
        P("member", "group"),
        P(both, None),
        P(both, None, None),
    )
    return jax.shard_map(
        local, mesh=mesh, in_specs=placed, out_specs=P(both, None), check_vma=False
    )
```

```python
import functools

import jax
import jax.numpy as jnp
from jax import lax
from jax.experimental import pallas as pl
from jax.experimental.pallas import tpu as pltpu
from jax.sharding import PartitionSpec as P

D = 4096
HQ = 64
KVH = 4
HD = 128
TOPP = 8
QLEN = 128
PLEN = 64
RECOMP = 16
KEPT = PLEN - RECOMP
EPSILON = 1e-06
LOG2E = 1.4426950408889634
MESH = pl.DeviceIdType.MESH
NX, NY, NZ = 4, 4, 8
HPB = 8
HPA = 4
PARTS = 4
PART = 2 * KVH * HD // PARTS
GROUPED = HQ // KVH
WIDTH = GROUPED * HD
FACTOR = LOG2E / HD**0.5


def comm_kernel(
    ret_ref, cache_ref, hid_hbm, w_ref, pos_hbm, q_hbm, own_hbm,
    slots_ref, rec_ref, part_ref, lse_ref,
    blk, wb, hn, acc, stage, recst, info, picks, hid_ref, pos_ref, queries, own_ref, ones, part, lse,
    local_sem, in_sem, q_sem, part_sem, lse_sem, keep_sem, wz_s, wz_r, wy_s, wy_r, wx_s, wx_r, wf_s, wf_r,
    in_s, in_r, zr_s, zr_r, zl_s, zl_r, ys_s, ys_r, hx_s, hx_r, rx_s, rx_r,
):
    g, m = lax.axis_index("group"), lax.axis_index("member")
    x, c, y, z = g // 2, g % 2, m // NZ, m % NZ

    def at(dx=0, dc=0, dy=0, dz=0):
        gg = ((x + dx + NX) % NX) * 2 + (c + dc) % 2
        return gg, ((y + dy + NY) % NY) * NZ + (z + dz + NZ) % NZ

    def remote(src, dst, s, r, dev):
        return pltpu.make_async_remote_copy(
            src_ref=src, dst_ref=dst, send_sem=s, recv_sem=r, device_id=dev, device_id_type=MESH
        )

    sends = []

    def go(copy):
        copy.start()
        sends.append(copy)
        return copy

    loads = [
        pltpu.make_async_copy(src, dst, in_sem.at[i])
        for i, (src, dst) in enumerate(((pos_hbm, pos_ref), (own_hbm, own_ref), (hid_hbm, hid_ref)))
    ]

    def query(n, h):
        block = (pl.ds(n * QLEN, QLEN), pl.ds(h * WIDTH, WIDTH))
        return pltpu.make_async_copy(q_hbm.at[block], queries.at[block], q_sem.at[n, h])

    peers = [at(dz=k) for k in range(1, NZ)] + [at(dy=k) for k in range(1, NY)]
    peers += [at(dx=1), at(dx=-1), at(dc=1)]
    barrier = pltpu.get_barrier_semaphore()
    for dev in peers:
        pl.semaphore_signal(barrier, inc=1, device_id=dev, device_id_type=MESH)

    for copy in loads:
        copy.start()
    for n in range(2):
        for h in range(KVH):
            query(n, h).start()

    lane = lax.broadcasted_iota(jnp.int32, (16, 256), 1)
    row = lane % PLEN
    loads[0].wait()
    spots = pos_ref[...].reshape(16, RECOMP)
    covered = row == spots[:, 0:1]
    for j in range(1, RECOMP):
        covered = covered | (row == spots[:, j : j + 1])
    free = jnp.where(covered[:, :PLEN], 0.0, 1.0).astype(jnp.bfloat16)
    below = lax.broadcasted_iota(jnp.int32, (PLEN, 256), 0)
    before = below < lax.broadcasted_iota(jnp.int32, (PLEN, 256), 1) % PLEN
    rank = jnp.dot(
        free, jnp.where(before, 1.0, 0.0).astype(jnp.bfloat16), preferred_element_type=jnp.float32
    )
    request = lax.broadcasted_iota(jnp.int32, (16, 256), 0)
    wanted = jnp.zeros((16, 256), jnp.int32)
    for k in range(16):
        wanted = jnp.where(request == k, ret_ref[k // TOPP, k % TOPP], wanted)
    keep = jnp.logical_not(covered) & (lane // PLEN == wanted % 4)
    info[0, :, 0:256] = jnp.where(keep, rank, -1.0)
    info[0, :, 256:512] = (wanted // 4).astype(jnp.float32)

    pl.semaphore_wait(barrier, len(peers))

    zrow = pl.multiple_of(z * 128, 128)
    for k in range(1, NZ):
        dst = wb.at[x, y, pl.ds(zrow, 128)]
        go(remote(w_ref, dst, wz_s.at[k], wz_r.at[k], at(dz=k)))
    for k in range(1, NY):
        go(remote(info.at[0], info.at[k], in_s.at[k], in_r.at[k], at(dy=k)))

    last = 3 * PARTS

    def part_right(i):
        return i % PARTS

    def part_left(i):
        return PARTS - 1 - i % PARTS

    def zz(d):
        return (z + d + NZ) % NZ

    def own_part(h):
        return cache_ref.at[:, pl.ds(h * PART, PART)]

    def right(i):
        h = part_right(i)
        dst = blk.at[zz(-(i // PARTS)), h]
        return remote(own_part(h) if i < PARTS else dst, dst, zr_s.at[i], zr_r.at[i], at(dz=1))

    def left(i):
        h = part_left(i)
        dst = blk.at[zz(i // PARTS), h]
        return remote(own_part(h) if i < PARTS else dst, dst, zl_s.at[i], zl_r.at[i], at(dz=-1))

    def z_arrived(i):
        d = blk.at[zz(-1 - i // PARTS), part_right(i)]
        remote(d, d, zr_s.at[i], zr_r.at[i], at(dz=-1)).wait_recv()
        if i + PARTS < last + PARTS // 2:
            go(right(i + PARTS))
        d = blk.at[zz(1 + i // PARTS), part_left(i)]
        remote(d, d, zl_s.at[i], zl_r.at[i], at(dz=1)).wait_recv()
        if i + PARTS < last + PARTS // 2:
            go(left(i + PARTS))
        select(-1 - i // PARTS, part_right(i))
        select(1 + i // PARTS, part_left(i))

    own_w = pltpu.make_async_copy(w_ref, wb.at[x, y, pl.ds(zrow, 128)], local_sem.at[1])
    own_w.start()
    own_block = [
        pltpu.make_async_copy(own_part(h), blk.at[z, h], local_sem.at[2 + h])
        for h in range(PARTS)
    ]
    for copy in own_block:
        copy.start()

    loads[2].wait()
    def norm(i, carry):
        rows = pl.ds(pl.multiple_of(i * 32, 32), 32)
        h = hid_ref[rows, :].astype(jnp.float32)
        inv = lax.rsqrt(jnp.mean(h * h, axis=1, keepdims=True) + EPSILON)
        n = (h * inv).astype(jnp.bfloat16)
        for b in range(4):
            hn[b, rows, :] = n[:, b * 1024 : (b + 1) * 1024]
        return carry

    lax.fori_loop(0, 8, norm, 0)
    mine, theirs = pl.ds(0, 256), pl.ds(256, 256)
    go(remote(hn.at[:, mine], hn.at[:, theirs], hx_s, hx_r, at(dc=1)))

    for i in range(PARTS):
        go(right(i))
        go(left(i))

    def w_row(k):
        return wb.at[x, y, pl.ds(pl.multiple_of(zz(-k) * 128, 128), 128)]

    def wz_arrived(k):
        d = w_row(k)
        remote(d, d, wz_s.at[k], wz_r.at[k], at(dz=-k if k < 4 else NZ - k)).wait_recv()

    def wz_forward(k, steps):
        j = (k + steps) % NZ
        go(remote(w_row(k), w_row(k), wz_s.at[j], wz_r.at[j], at(dz=steps)))


    local = []

    def choose(d):
        name = (y * NZ + zz(d)).astype(jnp.float32)
        want = lax.broadcasted_iota(jnp.int32, (KEPT, 256), 0).astype(jnp.float32)
        for k in range(NY):
            hit = info[k, :, 256:512] == name
            v = jnp.max(jnp.where(hit, info[k, :, 0:256], -1.0), axis=0, keepdims=True)
            picks[d % NZ, k * KEPT : (k + 1) * KEPT] = jnp.where(want == v, 1.0, 0.0).astype(
                jnp.bfloat16
            )

    def select(d, h):
        holder, e = zz(d), d % NZ
        got = jnp.dot(picks[e], blk[holder, h], preferred_element_type=jnp.float32)
        got = got.astype(jnp.bfloat16)
        for k in range(NY):
            stage[k, e, h] = got[k * KEPT : (k + 1) * KEPT]
        slot = slots_ref.at[y * NZ + holder, h]
        for k in range(1, NY):
            remote(stage.at[k, e, h], slot, ys_s.at[k], ys_r.at[k], at(dy=-k)).start()
        pltpu.make_async_copy(stage.at[0, e, h], slot, keep_sem).start()

    started = set()

    def project(dx, k):
        xi, yi = (x + dx + NX) % NX, (y - k + NY) % NY
        part = jnp.dot(hn[yi], wb[xi, yi], preferred_element_type=jnp.float32)
        if dx in started:
            acc[dx] = acc[dx] + part
        else:
            started.add(dx)
            acc[dx] = part

    def chunk(dx, k):
        return wb.at[(x + dx + NX) % NX, (y - k + NY) % NY]

    def wx_send(k):
        go(remote(chunk(0, k), chunk(0, k), wx_s.at[0, k], wx_r.at[0, k], at(dx=1)))
        go(remote(chunk(0, k), chunk(0, k), wx_s.at[1, k], wx_r.at[1, k], at(dx=-1)))

    def wx_arrived(k):
        d = chunk(-1, k)
        remote(d, d, wx_s.at[0, k], wx_r.at[0, k], at(dx=-1)).wait_recv()
        if k in (0, 1):
            go(remote(d, d, wf_s.at[k], wf_r.at[k], at(dx=1)))
        d = chunk(1, k)
        remote(d, d, wx_s.at[1, k], wx_r.at[1, k], at(dx=1)).wait_recv()
        if k in (2, 3):
            go(remote(d, d, wf_s.at[k], wf_r.at[k], at(dx=-1)))
        project(3, k)
        project(1, k)

    def wf_arrived(k):
        d = chunk(2, k)
        remote(d, d, wf_s.at[k], wf_r.at[k], at(dx=-1 if k in (0, 1) else 1)).wait_recv()
        project(2, k)

    def wy_arrived(k):
        d = chunk(0, k)
        remote(d, d, wy_s.at[k], wy_r.at[k], at(dy=-k)).wait_recv()
        wx_send(k)
        project(0, k)

    loads[1].wait()
    ones[:, HD:] = jnp.ones((QLEN, HD), jnp.bfloat16)
    token = lax.broadcasted_iota(jnp.int32, (HPB * QLEN, QLEN), 0) % QLEN
    seen = lax.broadcasted_iota(jnp.int32, (HPB * QLEN, QLEN), 1) <= token

    def attend_own(n, h):
        query(n, h).wait()
        rows = slice(n * QLEN, (n + 1) * QLEN)
        key = own_ref[rows, h * HD : (h + 1) * HD]
        ones[:, :HD] = own_ref[rows, (KVH + h) * HD : (KVH + h + 1) * HD]
        for b in range(GROUPED // HPB):
            cols = [h * WIDTH + (b * HPB + i) * HD for i in range(HPB)]
            q = jnp.concatenate([queries[rows, a : a + HD] for a in cols], axis=0)
            s = lax.dot_general(q, key, (((1,), (1,)), ((), ())), preferred_element_type=jnp.float32)
            s = jnp.where(seen, s, -jnp.inf)
            peak = jnp.max(s, axis=1, keepdims=True)
            p = jnp.exp2((s - peak) * FACTOR).astype(jnp.bfloat16)
            o = jnp.dot(p, ones[...], preferred_element_type=jnp.float32)
            total = o[:, HD:]
            o = (o[:, :HD] / total).astype(jnp.bfloat16)
            score = peak + jnp.log2(total) / FACTOR
            for i, a in enumerate(cols):
                part[rows, a : a + HD] = o[i * QLEN : (i + 1) * QLEN]
                lse[rows, a : a + HD] = score[i * QLEN : (i + 1) * QLEN]
        block = (pl.ds(n * QLEN, QLEN), pl.ds(h * WIDTH, WIDTH))
        for copy in (
            pltpu.make_async_copy(part.at[block], part_ref.at[block], part_sem.at[n, h]),
            pltpu.make_async_copy(lse.at[block], lse_ref.at[block], lse_sem.at[n, h]),
        ):
            copy.start()
            local.append(copy)

    for k in range(1, NY):
        remote(info.at[k], info.at[k], in_s.at[k], in_r.at[k], at(dy=-k)).wait_recv()
    for d in range(NZ):
        choose(d)
    for copy in own_block:
        copy.wait()
    for h in range(PARTS):
        select(0, h)
    attend_own(0, 0)

    own_w.wait()
    for k in range(1, NZ):
        wz_arrived(k)
    wx_send(0)
    for k in (1, 3):
        go(remote(chunk(0, 0), chunk(0, 0), wy_s.at[k], wy_r.at[k], at(dy=k)))
    remote(hn.at[:, mine], hn.at[:, theirs], hx_s, hx_r, at(dc=1)).wait_recv()
    project(0, 0)
    z_arrived(0)
    z_arrived(1)
    attend_own(0, 1)
    wx_arrived(0)
    wy_arrived(1)
    wy_arrived(3)
    go(remote(chunk(0, 0), chunk(0, 0), wy_s.at[2], wy_r.at[2], at(dy=2)))
    z_arrived(2)
    z_arrived(3)
    attend_own(0, 2)
    z_arrived(4)
    wf_arrived(0)
    attend_own(0, 3)
    z_arrived(5)
    wy_arrived(2)
    z_arrived(6)
    attend_own(1, 0)
    wx_arrived(1)
    z_arrived(7)
    attend_own(1, 1)
    z_arrived(8)
    wx_arrived(3)
    attend_own(1, 2)
    z_arrived(9)
    attend_own(1, 3)
    z_arrived(10)
    wx_arrived(2)
    z_arrived(11)
    wf_arrived(1)
    wf_arrived(3)
    z_arrived(12)
    wf_arrived(2)

    for dx in range(NX):
        xi = (x + dx) % NX
        recst[dx] = acc[dx].astype(jnp.bfloat16)
        dst = rec_ref.at[2 * xi + c]
        go(remote(recst.at[dx, theirs], dst, rx_s.at[dx], rx_r.at[dx], at(dc=1)))
        own = pltpu.make_async_copy(recst.at[dx, mine], dst, local_sem.at[12 + dx])
        own.start()
        local.append(own)

    z_arrived(13)

    for dx in range(NX):
        dst = rec_ref.at[2 * ((x + dx) % NX) + (c + 1) % 2]
        remote(recst.at[dx, theirs], dst, rx_s.at[dx], rx_r.at[dx], at(dc=1)).wait_recv()
    for copy in local:
        copy.wait()
    for copy in sends:
        copy.wait_send()
    pltpu.make_async_copy(stage.at[0], slots_ref.at[pl.ds(y * NZ, NZ)], keep_sem).wait()
    for k in range(1, NY):
        rows = slots_ref.at[pl.ds((y + k) % NY * NZ, NZ)]
        remote(stage.at[k], rows, ys_s.at[k], ys_r.at[k], at(dy=-k)).wait_send()
        remote(stage.at[k], rows, ys_s.at[k], ys_r.at[k], at(dy=k)).wait_recv()


def attend_kernel(
    ret_ref, q_hbm, part_hbm, lse_hbm, slots_hbm, rec_hbm, out_hbm,
    ctx, vals, queries, part, lse, out, sem, q_sem, part_sem, lse_sem, out_sem,
):
    cached, steps = TOPP * KEPT, 2 * KVH

    def fetch(i):
        copies = [
            pltpu.make_async_copy(
                slots_hbm.at[ret_ref[i, j] // 4], ctx.at[i, :, pl.ds(j * KEPT, KEPT)], sem.at[i, j]
            )
            for j in range(TOPP)
        ]
        return copies + [
            pltpu.make_async_copy(
                rec_hbm.at[e, pl.ds(i * QLEN, QLEN)],
                ctx.at[i, e // 2, pl.ds(cached, QLEN), pl.ds(e % 2 * HD, HD)],
                sem.at[i, TOPP + e],
            )
            for e in range(2 * KVH)
        ]

    def block(t):
        row = pl.multiple_of(t // KVH * QLEN, QLEN)
        col = pl.multiple_of(t % KVH * WIDTH, WIDTH)
        return pl.ds(row, QLEN), pl.ds(col, WIDTH)

    def inputs(t):
        return [
            pltpu.make_async_copy(src.at[block(t)], dst.at[block(t)], s.at[t])
            for src, dst, s in (
                (q_hbm, queries, q_sem), (part_hbm, part, part_sem), (lse_hbm, lse, lse_sem),
            )
        ]

    def output(t):
        return pltpu.make_async_copy(out.at[block(t)], out_hbm.at[block(t)], out_sem.at[t])

    for copy in fetch(0) + inputs(0):
        copy.start()
    vals[:, HD:] = jnp.ones((TOPP * PLEN, HD), jnp.bfloat16)
    for copy in fetch(0):
        copy.wait()
    for copy in inputs(1):
        copy.start()

    def step(t, carry):
        for copy in inputs(t):
            copy.wait()

        @pl.when(t < steps - 2)
        def _():
            for copy in inputs(t + 2):
                copy.start()

        @pl.when(t == 1)
        def _():
            for copy in fetch(1):
                copy.start()

        @pl.when(t == KVH)
        def _():
            for copy in fetch(1):
                copy.wait()

        n, h = t // KVH, t % KVH
        rows = pl.ds(pl.multiple_of(n * QLEN, QLEN), QLEN)
        head = pl.ds(pl.multiple_of(h % 2 * HD, HD), HD)
        key = ctx[n, h // 2, :, head]
        vals[:, :HD] = ctx[n, 2 + h // 2, :, head]

        def cols(b, i):
            return pl.ds(pl.multiple_of(h * WIDTH + (b * HPA + i) * HD, HD), HD)

        def stack(ref, b):
            return jnp.concatenate([ref[rows, cols(b, i)] for i in range(HPA)], axis=0)

        def score(b):
            return lax.dot_general(
                stack(queries, b), key, (((1,), (1,)), ((), ())), preferred_element_type=jnp.float32
            )

        def finish(b, s):
            own = stack(lse, b)
            peak = jnp.maximum(jnp.max(s, axis=1, keepdims=True), own)
            p = jnp.concatenate(
                [
                    jnp.exp2((s[:, c : c + HD] - peak) * FACTOR).astype(jnp.bfloat16)
                    for c in range(0, TOPP * PLEN, HD)
                ],
                axis=1,
            )
            weight = jnp.exp2((own - peak) * FACTOR)
            o = jnp.dot(p, vals[...], preferred_element_type=jnp.float32)
            top = o[:, :HD] + weight * stack(part, b).astype(jnp.float32)
            o = (top / (o[:, HD:] + weight)).astype(jnp.bfloat16)
            for i in range(HPA):
                out[rows, cols(b, i)] = o[i * QLEN : (i + 1) * QLEN]

        groups = GROUPED // HPA
        s = score(0)
        for b in range(groups):
            later = score(b + 1) if b + 1 < groups else None
            finish(b, s)
            s = later
        output(t).start()
        return carry

    lax.fori_loop(0, steps, step, 0)
    for t in range(steps):
        output(t).wait()


def communicate(retrieval, cache, hidden, w_kv, positions, q, own):
    dma, bf, f32 = pltpu.SemaphoreType.DMA, jnp.bfloat16, jnp.float32
    hbm = pl.BlockSpec(memory_space=pltpu.HBM)
    return pl.pallas_call(
        comm_kernel,
        out_shape=(
            jax.ShapeDtypeStruct((NY * NZ, PARTS, KEPT, PART), bf),
            jax.ShapeDtypeStruct((8, 256, 128), bf),
            jax.ShapeDtypeStruct(q.shape, bf),
            jax.ShapeDtypeStruct(q.shape, f32),
        ),
        in_specs=[pl.BlockSpec(memory_space=pltpu.SMEM)] + [hbm] * 6,
        out_specs=(hbm,) * 4,
        scratch_shapes=[
            pltpu.VMEM((NZ, PARTS, 256, PART), bf),
            pltpu.VMEM((NX, NY, 1024, 128), bf),
            pltpu.VMEM((4, 512, 1024), bf),
            pltpu.VMEM((NX, 512, 128), f32),
            pltpu.VMEM((NY, NZ, PARTS, KEPT, PART), bf),
            pltpu.VMEM((NX, 512, 128), bf),
            pltpu.VMEM((NY, 16, 512), f32),
            pltpu.VMEM((NZ, NY * KEPT, 256), bf),
            pltpu.VMEM(hidden.shape, bf),
            pltpu.VMEM(positions.shape, jnp.int32),
            pltpu.VMEM(q.shape, bf),
            pltpu.VMEM(own.shape, bf),
            pltpu.VMEM((QLEN, 2 * HD), bf),
            pltpu.VMEM(q.shape, bf),
            pltpu.VMEM(q.shape, f32),
            dma((16,)), dma((3,)), dma((2, KVH)), dma((2, KVH)), dma((2, KVH)), dma,
            dma((NZ,)), dma((NZ,)), dma((NY,)), dma((NY,)),
            dma((2, NY)), dma((2, NY)), dma((NY,)), dma((NY,)),
            dma((NY,)), dma((NY,)), dma((14,)), dma((14,)), dma((14,)), dma((14,)),
            dma((NY,)), dma((NY,)), dma, dma, dma((NX,)), dma((NX,)),
        ],
        compiler_params=pltpu.CompilerParams(
            collective_id=0, has_side_effects=True, vmem_limit_bytes=56 << 20
        ),
        name="exchange",
    )(retrieval, cache, hidden, w_kv, positions, q, own)


def attend(retrieval, q, part, lse, slots, rec):
    dma, bf = pltpu.SemaphoreType.DMA, jnp.bfloat16
    hbm = pl.BlockSpec(memory_space=pltpu.HBM)
    return pl.pallas_call(
        attend_kernel,
        out_shape=jax.ShapeDtypeStruct(q.shape, q.dtype),
        in_specs=[pl.BlockSpec(memory_space=pltpu.SMEM)] + [hbm] * 5,
        out_specs=hbm,
        scratch_shapes=[
            pltpu.VMEM((2, PARTS, TOPP * PLEN, PART), bf),
            pltpu.VMEM((TOPP * PLEN, 2 * HD), bf),
            pltpu.VMEM(q.shape, bf),
            pltpu.VMEM(q.shape, bf),
            pltpu.VMEM(q.shape, jnp.float32),
            pltpu.VMEM(q.shape, bf),
            dma((2, TOPP + 2 * KVH)), dma((8,)), dma((8,)), dma((8,)), dma((8,)),
        ],
        compiler_params=pltpu.CompilerParams(vmem_limit_bytes=56 << 20),
        name="attend",
    )(retrieval, q, part, lse, slots, rec)


def local(q_rows, own_kv, cache, recomp_hidden, w_kv, retrieval, positions):
    slots, rec, part, lse = communicate(
        retrieval,
        cache.reshape(256, 1024),
        recomp_hidden.reshape(256, D),
        w_kv,
        positions,
        q_rows,
        own_kv,
    )
    return attend(retrieval, q_rows, part, lse, slots, rec)


def solution(mesh):
    both = ("group", "member")
    placed = (
        P(both, None),
        P(both, None),
        P(both, None, None),
        P(both, None, None, None),
        P("member", "group"),
        P(both, None),
        P(both, None, None),
    )
    return jax.shard_map(
        local, mesh=mesh, in_specs=placed, out_specs=P(both, None), check_vma=False
    )
```

```python
import functools

import jax
import jax.numpy as jnp
from jax import lax
from jax.experimental import pallas as pl
from jax.experimental.pallas import tpu as pltpu
from jax.sharding import PartitionSpec as P

D = 4096
HQ = 64
KVH = 4
HD = 128
TOPP = 8
QLEN = 128
PLEN = 64
RECOMP = 16
KEPT = PLEN - RECOMP
EPSILON = 1e-06
LOG2E = 1.4426950408889634
MESH = pl.DeviceIdType.MESH
NX, NY, NZ = 4, 4, 8
HPB = 8
HPA = 4
PARTS = 4
PART = 2 * KVH * HD // PARTS
GROUPED = HQ // KVH
WIDTH = GROUPED * HD
FACTOR = LOG2E / HD**0.5


def comm_kernel(
    ret_ref, cache_ref, hid_hbm, w_ref, pos_hbm, q_hbm, own_hbm,
    slots_ref, rec_ref, part_ref, lse_ref,
    blk, wb, hn, acc, stage, recst, info, picks, hid_ref, pos_ref, queries, own_ref, ones, part, lse,
    local_sem, in_sem, q_sem, part_sem, lse_sem, keep_sem, wz_s, wz_r, wy_s, wy_r, wx_s, wx_r, wf_s, wf_r,
    in_s, in_r, zr_s, zr_r, zl_s, zl_r, ys_s, ys_r, hx_s, hx_r, rx_s, rx_r,
):
    g, m = lax.axis_index("group"), lax.axis_index("member")
    x, c, y, z = g // 2, g % 2, m // NZ, m % NZ

    def at(dx=0, dc=0, dy=0, dz=0):
        gg = ((x + dx + NX) % NX) * 2 + (c + dc) % 2
        return gg, ((y + dy + NY) % NY) * NZ + (z + dz + NZ) % NZ

    def remote(src, dst, s, r, dev):
        return pltpu.make_async_remote_copy(
            src_ref=src, dst_ref=dst, send_sem=s, recv_sem=r, device_id=dev, device_id_type=MESH
        )

    sends = []

    def go(copy):
        copy.start()
        sends.append(copy)
        return copy

    loads = [
        pltpu.make_async_copy(src, dst, in_sem.at[i])
        for i, (src, dst) in enumerate(((pos_hbm, pos_ref), (own_hbm, own_ref), (hid_hbm, hid_ref)))
    ]

    def query(n, h):
        block = (pl.ds(n * QLEN, QLEN), pl.ds(h * WIDTH, WIDTH))
        return pltpu.make_async_copy(q_hbm.at[block], queries.at[block], q_sem.at[n, h])

    peers = [at(dz=k) for k in range(1, NZ)] + [at(dy=k) for k in range(1, NY)]
    peers += [at(dx=1), at(dx=-1), at(dc=1)]
    barrier = pltpu.get_barrier_semaphore()
    for dev in peers:
        pl.semaphore_signal(barrier, inc=1, device_id=dev, device_id_type=MESH)

    for copy in loads:
        copy.start()
    for n in range(2):
        for h in range(KVH):
            query(n, h).start()

    lane = lax.broadcasted_iota(jnp.int32, (16, 256), 1)
    row = lane % PLEN
    loads[0].wait()
    spots = pos_ref[...].reshape(16, RECOMP)
    covered = row == spots[:, 0:1]
    for j in range(1, RECOMP):
        covered = covered | (row == spots[:, j : j + 1])
    free = jnp.where(covered[:, :PLEN], 0.0, 1.0).astype(jnp.bfloat16)
    below = lax.broadcasted_iota(jnp.int32, (PLEN, 256), 0)
    before = below < lax.broadcasted_iota(jnp.int32, (PLEN, 256), 1) % PLEN
    rank = jnp.dot(
        free, jnp.where(before, 1.0, 0.0).astype(jnp.bfloat16), preferred_element_type=jnp.float32
    )
    request = lax.broadcasted_iota(jnp.int32, (16, 256), 0)
    wanted = jnp.zeros((16, 256), jnp.int32)
    for k in range(16):
        wanted = jnp.where(request == k, ret_ref[k // TOPP, k % TOPP], wanted)
    keep = jnp.logical_not(covered) & (lane // PLEN == wanted % 4)
    info[0, :, 0:256] = jnp.where(keep, rank, -1.0)
    info[0, :, 256:512] = (wanted // 4).astype(jnp.float32)

    pl.semaphore_wait(barrier, len(peers))

    zrow = pl.multiple_of(z * 128, 128)
    for k in range(1, NZ):
        dst = wb.at[x, y, pl.ds(zrow, 128)]
        go(remote(w_ref, dst, wz_s.at[k], wz_r.at[k], at(dz=k)))
    for k in range(1, NY):
        go(remote(info.at[0], info.at[k], in_s.at[k], in_r.at[k], at(dy=k)))

    last = 3 * PARTS

    def part_right(i):
        return i % PARTS

    def part_left(i):
        return PARTS - 1 - i % PARTS

    def zz(d):
        return (z + d + NZ) % NZ

    def own_part(h):
        return cache_ref.at[:, pl.ds(h * PART, PART)]

    def right(i):
        h = part_right(i)
        dst = blk.at[zz(-(i // PARTS)), h]
        return remote(own_part(h) if i < PARTS else dst, dst, zr_s.at[i], zr_r.at[i], at(dz=1))

    def left(i):
        h = part_left(i)
        dst = blk.at[zz(i // PARTS), h]
        return remote(own_part(h) if i < PARTS else dst, dst, zl_s.at[i], zl_r.at[i], at(dz=-1))

    def z_arrived(i):
        d = blk.at[zz(-1 - i // PARTS), part_right(i)]
        remote(d, d, zr_s.at[i], zr_r.at[i], at(dz=-1)).wait_recv()
        if i + PARTS < last + PARTS // 2:
            go(right(i + PARTS))
        d = blk.at[zz(1 + i // PARTS), part_left(i)]
        remote(d, d, zl_s.at[i], zl_r.at[i], at(dz=1)).wait_recv()
        if i + PARTS < last + PARTS // 2:
            go(left(i + PARTS))
        select(-1 - i // PARTS, part_right(i))
        select(1 + i // PARTS, part_left(i))

    own_w = pltpu.make_async_copy(w_ref, wb.at[x, y, pl.ds(zrow, 128)], local_sem.at[1])
    own_w.start()
    own_block = [
        pltpu.make_async_copy(own_part(h), blk.at[z, h], local_sem.at[2 + h])
        for h in range(PARTS)
    ]
    for copy in own_block:
        copy.start()

    loads[2].wait()
    def norm(i, carry):
        rows = pl.ds(pl.multiple_of(i * 32, 32), 32)
        h = hid_ref[rows, :].astype(jnp.float32)
        inv = lax.rsqrt(jnp.mean(h * h, axis=1, keepdims=True) + EPSILON)
        n = (h * inv).astype(jnp.bfloat16)
        for b in range(4):
            hn[b, rows, :] = n[:, b * 1024 : (b + 1) * 1024]
        return carry

    lax.fori_loop(0, 8, norm, 0)
    mine, theirs = pl.ds(0, 256), pl.ds(256, 256)
    go(remote(hn.at[:, mine], hn.at[:, theirs], hx_s, hx_r, at(dc=1)))

    for i in range(PARTS):
        go(right(i))
        go(left(i))

    def w_row(k):
        return wb.at[x, y, pl.ds(pl.multiple_of(zz(-k) * 128, 128), 128)]

    def wz_arrived(k):
        d = w_row(k)
        remote(d, d, wz_s.at[k], wz_r.at[k], at(dz=-k if k < 4 else NZ - k)).wait_recv()

    def wz_forward(k, steps):
        j = (k + steps) % NZ
        go(remote(w_row(k), w_row(k), wz_s.at[j], wz_r.at[j], at(dz=steps)))


    local = []

    def choose(d):
        name = (y * NZ + zz(d)).astype(jnp.float32)
        want = lax.broadcasted_iota(jnp.int32, (KEPT, 256), 0).astype(jnp.float32)
        for k in range(NY):
            hit = info[k, :, 256:512] == name
            v = jnp.max(jnp.where(hit, info[k, :, 0:256], -1.0), axis=0, keepdims=True)
            picks[d % NZ, k * KEPT : (k + 1) * KEPT] = jnp.where(want == v, 1.0, 0.0).astype(
                jnp.bfloat16
            )

    def select(d, h):
        holder, e = zz(d), d % NZ
        got = jnp.dot(picks[e], blk[holder, h], preferred_element_type=jnp.float32)
        got = got.astype(jnp.bfloat16)
        for k in range(NY):
            stage[k, e, h] = got[k * KEPT : (k + 1) * KEPT]
        slot = slots_ref.at[y * NZ + holder, h]
        for k in range(1, NY):
            remote(stage.at[k, e, h], slot, ys_s.at[k], ys_r.at[k], at(dy=-k)).start()
        pltpu.make_async_copy(stage.at[0, e, h], slot, keep_sem).start()

    started = set()

    def project(dx, k):
        xi, yi = (x + dx + NX) % NX, (y - k + NY) % NY
        part = jnp.dot(hn[yi], wb[xi, yi], preferred_element_type=jnp.float32)
        if dx in started:
            acc[dx] = acc[dx] + part
        else:
            started.add(dx)
            acc[dx] = part

    def chunk(dx, k):
        return wb.at[(x + dx + NX) % NX, (y - k + NY) % NY]

    def wx_send(k):
        go(remote(chunk(0, k), chunk(0, k), wx_s.at[0, k], wx_r.at[0, k], at(dx=1)))
        go(remote(chunk(0, k), chunk(0, k), wx_s.at[1, k], wx_r.at[1, k], at(dx=-1)))

    def wx_arrived(k):
        d = chunk(-1, k)
        remote(d, d, wx_s.at[0, k], wx_r.at[0, k], at(dx=-1)).wait_recv()
        if k in (0, 1):
            go(remote(d, d, wf_s.at[k], wf_r.at[k], at(dx=1)))
        d = chunk(1, k)
        remote(d, d, wx_s.at[1, k], wx_r.at[1, k], at(dx=1)).wait_recv()
        if k in (2, 3):
            go(remote(d, d, wf_s.at[k], wf_r.at[k], at(dx=-1)))
        project(3, k)
        project(1, k)

    def wf_arrived(k):
        d = chunk(2, k)
        remote(d, d, wf_s.at[k], wf_r.at[k], at(dx=-1 if k in (0, 1) else 1)).wait_recv()
        project(2, k)

    def wy_arrived(k):
        d = chunk(0, k)
        remote(d, d, wy_s.at[k], wy_r.at[k], at(dy=-k)).wait_recv()
        wx_send(k)
        project(0, k)

    loads[1].wait()
    ones[:, HD:] = jnp.ones((QLEN, HD), jnp.bfloat16)
    token = lax.broadcasted_iota(jnp.int32, (HPB * QLEN, QLEN), 0) % QLEN
    seen = lax.broadcasted_iota(jnp.int32, (HPB * QLEN, QLEN), 1) <= token

    def attend_own(n, h):
        query(n, h).wait()
        rows = slice(n * QLEN, (n + 1) * QLEN)
        key = own_ref[rows, h * HD : (h + 1) * HD]
        ones[:, :HD] = own_ref[rows, (KVH + h) * HD : (KVH + h + 1) * HD]
        for b in range(GROUPED // HPB):
            cols = [h * WIDTH + (b * HPB + i) * HD for i in range(HPB)]
            q = jnp.concatenate([queries[rows, a : a + HD] for a in cols], axis=0)
            s = lax.dot_general(q, key, (((1,), (1,)), ((), ())), preferred_element_type=jnp.float32)
            s = jnp.where(seen, s, -jnp.inf)
            peak = jnp.max(s, axis=1, keepdims=True)
            p = jnp.exp2((s - peak) * FACTOR).astype(jnp.bfloat16)
            o = jnp.dot(p, ones[...], preferred_element_type=jnp.float32)
            total = o[:, HD:]
            o = (o[:, :HD] / total).astype(jnp.bfloat16)
            score = peak + jnp.log2(total) / FACTOR
            for i, a in enumerate(cols):
                part[rows, a : a + HD] = o[i * QLEN : (i + 1) * QLEN]
                lse[rows, a : a + HD] = score[i * QLEN : (i + 1) * QLEN]
        block = (pl.ds(n * QLEN, QLEN), pl.ds(h * WIDTH, WIDTH))
        for copy in (
            pltpu.make_async_copy(part.at[block], part_ref.at[block], part_sem.at[n, h]),
            pltpu.make_async_copy(lse.at[block], lse_ref.at[block], lse_sem.at[n, h]),
        ):
            copy.start()
            local.append(copy)

    own_w.wait()
    for k in range(1, NZ):
        wz_arrived(k)
    wx_send(0)
    for k in (1, 3):
        go(remote(chunk(0, 0), chunk(0, 0), wy_s.at[k], wy_r.at[k], at(dy=k)))
    for k in range(1, NY):
        remote(info.at[k], info.at[k], in_s.at[k], in_r.at[k], at(dy=-k)).wait_recv()
    for d in range(NZ):
        choose(d)
    for copy in own_block:
        copy.wait()
    for h in range(PARTS):
        select(0, h)
    attend_own(0, 0)

    remote(hn.at[:, mine], hn.at[:, theirs], hx_s, hx_r, at(dc=1)).wait_recv()
    project(0, 0)
    z_arrived(0)
    z_arrived(1)
    attend_own(0, 1)
    wx_arrived(0)
    wy_arrived(1)
    wy_arrived(3)
    go(remote(chunk(0, 0), chunk(0, 0), wy_s.at[2], wy_r.at[2], at(dy=2)))
    z_arrived(2)
    z_arrived(3)
    attend_own(0, 2)
    z_arrived(4)
    wf_arrived(0)
    attend_own(0, 3)
    z_arrived(5)
    wy_arrived(2)
    z_arrived(6)
    attend_own(1, 0)
    wx_arrived(1)
    z_arrived(7)
    attend_own(1, 1)
    z_arrived(8)
    wx_arrived(3)
    attend_own(1, 2)
    z_arrived(9)
    attend_own(1, 3)
    z_arrived(10)
    wx_arrived(2)
    z_arrived(11)
    wf_arrived(1)
    wf_arrived(3)
    z_arrived(12)
    wf_arrived(2)

    for dx in range(NX):
        xi = (x + dx) % NX
        recst[dx] = acc[dx].astype(jnp.bfloat16)
        dst = rec_ref.at[2 * xi + c]
        go(remote(recst.at[dx, theirs], dst, rx_s.at[dx], rx_r.at[dx], at(dc=1)))
        own = pltpu.make_async_copy(recst.at[dx, mine], dst, local_sem.at[12 + dx])
        own.start()
        local.append(own)

    z_arrived(13)

    for dx in range(NX):
        dst = rec_ref.at[2 * ((x + dx) % NX) + (c + 1) % 2]
        remote(recst.at[dx, theirs], dst, rx_s.at[dx], rx_r.at[dx], at(dc=1)).wait_recv()
    for copy in local:
        copy.wait()
    for copy in sends:
        copy.wait_send()
    pltpu.make_async_copy(stage.at[0], slots_ref.at[pl.ds(y * NZ, NZ)], keep_sem).wait()
    for k in range(1, NY):
        rows = slots_ref.at[pl.ds((y + k) % NY * NZ, NZ)]
        remote(stage.at[k], rows, ys_s.at[k], ys_r.at[k], at(dy=-k)).wait_send()
        remote(stage.at[k], rows, ys_s.at[k], ys_r.at[k], at(dy=k)).wait_recv()


def attend_kernel(
    ret_ref, q_hbm, part_hbm, lse_hbm, slots_hbm, rec_hbm, out_hbm,
    ctx, vals, queries, part, lse, out, sem, q_sem, part_sem, lse_sem, out_sem,
):
    cached, steps = TOPP * KEPT, 2 * KVH

    def fetch(i):
        copies = [
            pltpu.make_async_copy(
                slots_hbm.at[ret_ref[i, j] // 4], ctx.at[i, :, pl.ds(j * KEPT, KEPT)], sem.at[i, j]
            )
            for j in range(TOPP)
        ]
        return copies + [
            pltpu.make_async_copy(
                rec_hbm.at[e, pl.ds(i * QLEN, QLEN)],
                ctx.at[i, e // 2, pl.ds(cached, QLEN), pl.ds(e % 2 * HD, HD)],
                sem.at[i, TOPP + e],
            )
            for e in range(2 * KVH)
        ]

    def block(t):
        row = pl.multiple_of(t // KVH * QLEN, QLEN)
        col = pl.multiple_of(t % KVH * WIDTH, WIDTH)
        return pl.ds(row, QLEN), pl.ds(col, WIDTH)

    def inputs(t):
        return [
            pltpu.make_async_copy(src.at[block(t)], dst.at[block(t)], s.at[t])
            for src, dst, s in (
                (q_hbm, queries, q_sem), (part_hbm, part, part_sem), (lse_hbm, lse, lse_sem),
            )
        ]

    def output(t):
        return pltpu.make_async_copy(out.at[block(t)], out_hbm.at[block(t)], out_sem.at[t])

    for copy in fetch(0) + inputs(0):
        copy.start()
    vals[:, HD:] = jnp.ones((TOPP * PLEN, HD), jnp.bfloat16)
    for copy in fetch(0):
        copy.wait()
    for copy in inputs(1):
        copy.start()

    def step(t, carry):
        for copy in inputs(t):
            copy.wait()

        @pl.when(t < steps - 2)
        def _():
            for copy in inputs(t + 2):
                copy.start()

        @pl.when(t == 1)
        def _():
            for copy in fetch(1):
                copy.start()

        @pl.when(t == KVH)
        def _():
            for copy in fetch(1):
                copy.wait()

        n, h = t // KVH, t % KVH
        rows = pl.ds(pl.multiple_of(n * QLEN, QLEN), QLEN)
        head = pl.ds(pl.multiple_of(h % 2 * HD, HD), HD)
        key = ctx[n, h // 2, :, head]
        vals[:, :HD] = ctx[n, 2 + h // 2, :, head]

        def cols(b, i):
            return pl.ds(pl.multiple_of(h * WIDTH + (b * HPA + i) * HD, HD), HD)

        def stack(ref, b):
            return jnp.concatenate([ref[rows, cols(b, i)] for i in range(HPA)], axis=0)

        def score(b):
            return lax.dot_general(
                stack(queries, b), key, (((1,), (1,)), ((), ())), preferred_element_type=jnp.float32
            )

        def finish(b, s):
            own = stack(lse, b)
            peak = jnp.maximum(jnp.max(s, axis=1, keepdims=True), own)
            p = jnp.concatenate(
                [
                    jnp.exp2((s[:, c : c + HD] - peak) * FACTOR).astype(jnp.bfloat16)
                    for c in range(0, TOPP * PLEN, HD)
                ],
                axis=1,
            )
            weight = jnp.exp2((own - peak) * FACTOR)
            o = jnp.dot(p, vals[...], preferred_element_type=jnp.float32)
            top = o[:, :HD] + weight * stack(part, b).astype(jnp.float32)
            o = (top / (o[:, HD:] + weight)).astype(jnp.bfloat16)
            for i in range(HPA):
                out[rows, cols(b, i)] = o[i * QLEN : (i + 1) * QLEN]

        groups = GROUPED // HPA
        s = score(0)
        for b in range(groups):
            later = score(b + 1) if b + 1 < groups else None
            finish(b, s)
            s = later
        output(t).start()
        return carry

    lax.fori_loop(0, steps, step, 0)
    for t in range(steps):
        output(t).wait()


def communicate(retrieval, cache, hidden, w_kv, positions, q, own):
    dma, bf, f32 = pltpu.SemaphoreType.DMA, jnp.bfloat16, jnp.float32
    hbm = pl.BlockSpec(memory_space=pltpu.HBM)
    return pl.pallas_call(
        comm_kernel,
        out_shape=(
            jax.ShapeDtypeStruct((NY * NZ, PARTS, KEPT, PART), bf),
            jax.ShapeDtypeStruct((8, 256, 128), bf),
            jax.ShapeDtypeStruct(q.shape, bf),
            jax.ShapeDtypeStruct(q.shape, f32),
        ),
        in_specs=[pl.BlockSpec(memory_space=pltpu.SMEM)] + [hbm] * 6,
        out_specs=(hbm,) * 4,
        scratch_shapes=[
            pltpu.VMEM((NZ, PARTS, 256, PART), bf),
            pltpu.VMEM((NX, NY, 1024, 128), bf),
            pltpu.VMEM((4, 512, 1024), bf),
            pltpu.VMEM((NX, 512, 128), f32),
            pltpu.VMEM((NY, NZ, PARTS, KEPT, PART), bf),
            pltpu.VMEM((NX, 512, 128), bf),
            pltpu.VMEM((NY, 16, 512), f32),
            pltpu.VMEM((NZ, NY * KEPT, 256), bf),
            pltpu.VMEM(hidden.shape, bf),
            pltpu.VMEM(positions.shape, jnp.int32),
            pltpu.VMEM(q.shape, bf),
            pltpu.VMEM(own.shape, bf),
            pltpu.VMEM((QLEN, 2 * HD), bf),
            pltpu.VMEM(q.shape, bf),
            pltpu.VMEM(q.shape, f32),
            dma((16,)), dma((3,)), dma((2, KVH)), dma((2, KVH)), dma((2, KVH)), dma,
            dma((NZ,)), dma((NZ,)), dma((NY,)), dma((NY,)),
            dma((2, NY)), dma((2, NY)), dma((NY,)), dma((NY,)),
            dma((NY,)), dma((NY,)), dma((14,)), dma((14,)), dma((14,)), dma((14,)),
            dma((NY,)), dma((NY,)), dma, dma, dma((NX,)), dma((NX,)),
        ],
        compiler_params=pltpu.CompilerParams(
            collective_id=0, has_side_effects=True, vmem_limit_bytes=56 << 20
        ),
        name="exchange",
    )(retrieval, cache, hidden, w_kv, positions, q, own)


def attend(retrieval, q, part, lse, slots, rec):
    dma, bf = pltpu.SemaphoreType.DMA, jnp.bfloat16
    hbm = pl.BlockSpec(memory_space=pltpu.HBM)
    return pl.pallas_call(
        attend_kernel,
        out_shape=jax.ShapeDtypeStruct(q.shape, q.dtype),
        in_specs=[pl.BlockSpec(memory_space=pltpu.SMEM)] + [hbm] * 5,
        out_specs=hbm,
        scratch_shapes=[
            pltpu.VMEM((2, PARTS, TOPP * PLEN, PART), bf),
            pltpu.VMEM((TOPP * PLEN, 2 * HD), bf),
            pltpu.VMEM(q.shape, bf),
            pltpu.VMEM(q.shape, bf),
            pltpu.VMEM(q.shape, jnp.float32),
            pltpu.VMEM(q.shape, bf),
            dma((2, TOPP + 2 * KVH)), dma((8,)), dma((8,)), dma((8,)), dma((8,)),
        ],
        compiler_params=pltpu.CompilerParams(vmem_limit_bytes=56 << 20),
        name="attend",
    )(retrieval, q, part, lse, slots, rec)


def local(q_rows, own_kv, cache, recomp_hidden, w_kv, retrieval, positions):
    slots, rec, part, lse = communicate(
        retrieval,
        cache.reshape(256, 1024),
        recomp_hidden.reshape(256, D),
        w_kv,
        positions,
        q_rows,
        own_kv,
    )
    return attend(retrieval, q_rows, part, lse, slots, rec)


def solution(mesh):
    both = ("group", "member")
    placed = (
        P(both, None),
        P(both, None),
        P(both, None, None),
        P(both, None, None, None),
        P("member", "group"),
        P(both, None),
        P(both, None, None),
    )
    return jax.shard_map(
        local, mesh=mesh, in_specs=placed, out_specs=P(both, None), check_vma=False
    )
```
